128 devices in a mesh: seq: 32 (over x, y, core), head: 4 (over z).
Axes of the slice: x: 4, y: 4, z: 4, core: 2. Of those that a mesh axis runs over, the one named last changes fastest.
Arguments:
- queries: bfloat16 [2, 8192, 20, 128], P(None, ('seq', 'head')), may hold values from -96 to 96
- grad_out: bfloat16 [2, 8192, 20, 128], P(None, ('seq', 'head')), may hold values from -6 to 6
- keys: bfloat16 [8192, 4, 128], P('seq', 'head'), may hold values from -6 to 6
- values: bfloat16 [8192, 4, 128], P('seq', 'head'), may hold values from -6 to 6
- doc_start: int32 [8192], replicated, may hold values from 0 to 8191, as said below
Outputs:
- query_grads: bfloat16 [2, 8192, 20, 128], P(None, ('seq', 'head'))
- key_grads: bfloat16 [8192, 4, 128], P('seq', 'head')
- value_grads: bfloat16 [8192, 4, 128], P('seq', 'head')
The draws below stay inside these ranges and needn't reach their ends.
Inputs may be any that keep to these rules, and one draw needn't show every extreme that they name: doc_start[i] is the first position of token i's document, so doc_start[i] <= i; it is 0 for every token before position 4096, at most four documents begin at or after it, and the last token begins a document of its own.
All inputs are finite; a program needn't handle non-finite values.
Results may differ from the reference program's by a relative error of at most 0.005.
Values may be sent and summed in bfloat16 or wider, within the bound.
A program may use at most 128 MiB of HBM per device.

```python
import math
import jax
import jax.numpy as jnp
from jax import lax

H = 20
KVH = 4
DH = 128
L = 2
S = 8192


def draw_shared(key):
    base_key = jax.random.fold_in(key, 17)
    query_key, keys_key = jax.random.split(base_key, 2)
    key_rows = jax.random.normal(keys_key, (S, KVH, DH), jnp.float32)
    query_rows = jax.random.normal(query_key, (L, S, H, DH), jnp.float32)
    return (jnp.clip(query_rows, -96.0, 96.0), jnp.clip(key_rows, -6.0, 6.0))


def draw_queries(key, part):
    return draw_shared(key)[0].astype(jnp.bfloat16)


def draw_keys(key, part):
    return draw_shared(key)[1].astype(jnp.bfloat16)


def draw_doc_start(key, part):
    drawn = jax.random.randint(jax.random.fold_in(key, 29), (3,), S // 2, S - 1)
    starts = jnp.concatenate((drawn.astype(jnp.int32), jnp.full((1,), S - 1, jnp.int32)))
    positions = jnp.arange(S, dtype=jnp.int32)
    chosen = jnp.where(starts[None, :] <= positions[:, None], starts[None, :], 0)
    return jnp.max(chosen, axis=1).astype(jnp.int32)


def shard_levels(key, shape, cuts, smallest, top_value):
    def one(dim, shards_of):
        steps = jax.random.uniform(jax.random.fold_in(jax.random.fold_in(key, 6), dim), (shards_of,), jnp.float32, smallest / len(cuts), top_value / len(cuts))
        return jnp.repeat(jnp.exp(steps), shape[dim] // shards_of).reshape((-1,) + (1,) * (len(shape) - dim - 1))

    factor_of = one(*cuts[0])
    for cut in cuts[1:]:
        factor_of = factor_of * one(*cut)
    return factor_of


def gaussian(key, shape, deviation, reach, shards=(), kind=jnp.bfloat16):
    result = deviation * jax.random.normal(key, shape, jnp.float32)
    if shards:
        result = result * shard_levels(key, shape, shards, -0.22, 0.18)
    return jnp.clip(result, -reach, reach).astype(kind)


def setup_inputs(seed: int = 0) -> dict:
    arg_keys = jax.random.split(jax.random.key(seed), 6)
    queries = draw_queries(jax.random.fold_in(arg_keys[5], 71), 0)
    grad_out = gaussian(arg_keys[1], (L, S, H, DH), 1.0, 6.0, ((1, 128),))
    keys = draw_keys(jax.random.fold_in(arg_keys[5], 71), 0)
    values = gaussian(arg_keys[3], (S, KVH, DH), 1.0, 6.0, ((0, 32), (1, 4)))
    doc_start = draw_doc_start(jax.random.fold_in(arg_keys[5], 71), 0)
    return {"queries": queries, "grad_out": grad_out, "keys": keys, "values": values, "doc_start": doc_start}


def head_terms(query, grad, key_rows, value_rows, allowed, score_scale):
    scores = jnp.dot(query, key_rows.T, preferred_element_type=jnp.float32) * score_scale
    scores = jnp.where(allowed, scores, -jnp.inf)
    row_max = lax.optimization_barrier(jnp.max(scores, axis=1, keepdims=True))
    raw_weights = jnp.exp(scores - row_max)
    row_sum = lax.optimization_barrier(jnp.sum(raw_weights, axis=1, keepdims=True))
    grad_probs = jnp.dot(grad, value_rows.T, preferred_element_type=jnp.float32)
    row_delta = lax.optimization_barrier(jnp.sum(raw_weights * grad_probs, axis=1, keepdims=True)) / row_sum
    prob_rows = jnp.exp(scores - (row_max + jnp.log(row_sum)))
    grad_scores = prob_rows * (grad_probs - row_delta)
    grad_low = grad_scores.astype(jnp.bfloat16)
    prob_low = prob_rows.astype(jnp.bfloat16)
    query_part = (jnp.dot(grad_low, key_rows, preferred_element_type=jnp.float32) * score_scale).astype(jnp.bfloat16)
    key_part = jnp.dot(grad_low.T, query, preferred_element_type=jnp.float32)
    value_part = jnp.dot(prob_low.T, grad, preferred_element_type=jnp.float32)
    return (query_part, key_part, value_part)

def reference(queries, grad_out, keys, values, doc_start):
    positions = jnp.arange(S, dtype=jnp.int32)
    allowed = (positions[None, :] >= doc_start[:, None]) & (positions[None, :] <= positions[:, None])
    group_size = H // KVH
    score_scale = 1.0 / math.sqrt(DH)
    key_heads = jnp.repeat(jnp.moveaxis(keys, 1, 0), group_size, axis=0)
    value_heads = jnp.repeat(jnp.moveaxis(values, 1, 0), group_size, axis=0)
    layer_grads = []
    key_total = jnp.zeros((KVH, S, DH), jnp.float32)
    value_total = jnp.zeros((KVH, S, DH), jnp.float32)
    for layer_index in range(L):
        query_heads = jnp.moveaxis(queries[layer_index], 1, 0)
        grad_heads = jnp.moveaxis(grad_out[layer_index], 1, 0)
        query_part, key_part, value_part = lax.map(lambda packed: head_terms(packed[0], packed[1], packed[2], packed[3], allowed, score_scale), (query_heads, grad_heads, key_heads, value_heads))
        layer_grads.append(jnp.moveaxis(query_part, 0, 1))
        key_total = key_total + lax.optimization_barrier(jnp.sum(key_part.reshape(KVH, group_size, S, DH), axis=1))
        value_total = value_total + lax.optimization_barrier(jnp.sum(value_part.reshape(KVH, group_size, S, DH), axis=1))
    query_grads = jnp.stack(layer_grads, axis=0)
    key_grads = (jnp.moveaxis(key_total, 0, 1) * score_scale).astype(jnp.bfloat16)
    value_grads = jnp.moveaxis(value_total, 0, 1).astype(jnp.bfloat16)
    return (query_grads, key_grads, value_grads)
```

```python
import functools
import math

import jax
import jax.numpy as jnp
from jax import lax
from jax.experimental import pallas as pl
from jax.experimental.pallas import tpu as pltpu
from jax.sharding import PartitionSpec as P

NEG = -1e30
ROUNDS = 10
BK = 1024
MESH = pl.DeviceIdType.MESH
NT = (((1,), (1,)), ((), ()))
TN = (((0,), (0,)), ((), ()))
ANY = pl.BlockSpec(memory_space=pl.ANY)
VM = pl.BlockSpec(memory_space=pltpu.VMEM)


def coords():
    s = lax.axis_index("seq")
    z = lax.axis_index("head")
    c = lax.rem(s, 2)
    y = lax.rem(s // 2, 4)
    x = s // 8
    return s, z, x, y, c


def seq_of(x, y, c):
    return (x * 4 + y) * 2 + c


def wrap(v):
    return lax.rem(v + 4, 4)


def unit_dest(n):
    r = n // 32
    p = lax.rem(n, 32)
    return r, jnp.where(lax.rem(r, 2) == 0, p, 31 - p)


def unit_at(r, s):
    return 32 * r + jnp.where(lax.rem(r, 2) == 0, s, 31 - s)


def at_dev(s, z):
    return {"seq": s, "head": z}


def gather_kernel(qh, gh, k, v, qbuf, gbuf, kfull, vfull, qsend, gsend, qrecv, grecv, ksend, vsend, krecv, vrecv, kpart, vpart, lsem):
    s, z, x, y, c = coords()
    half = lax.rem(z, 2)
    blk = 2 * s + z // 2
    dests = []
    for h in range(5):
        r, ds = unit_dest(5 * blk + h)
        for g in range(4):
            dests.append((h, g, r, ds))
    sources = []
    for r in range(ROUNDS):
        b = unit_at(r, s) // 5
        for hf in range(2):
            sources.append((b // 2, 2 * lax.rem(b, 2) + hf))

    barrier = pltpu.get_barrier_semaphore()
    selfs = jnp.int32(0)
    for ss, sz in sources:
        mine = jnp.logical_and(ss == s, sz == z)

        @pl.when(jnp.logical_not(mine))
        def _():
            pl.semaphore_signal(barrier, inc=1, device_id=at_dev(ss, sz), device_id_type=MESH)

        selfs = selfs + mine.astype(jnp.int32)
    ring = [(1, 0), (-1, 0), (0, 1), (0, -1)]
    for dx, dy in ring:
        pl.semaphore_signal(barrier, inc=1, device_id=at_dev(seq_of(wrap(x + dx), wrap(y + dy), c), z), device_id_type=MESH)
    pl.semaphore_signal(barrier, inc=1, device_id=at_dev(seq_of(x, y, 1 - c), z), device_id_type=MESH)
    pl.semaphore_wait(barrier, 25 - selfs)

    own = [
        pltpu.make_async_copy(k, kfull.at[s], lsem.at[0]),
        pltpu.make_async_copy(v, vfull.at[s], lsem.at[1]),
    ]
    for d in own:
        d.start()

    order = [(0, 0), (-1, 0), (1, 0), (0, -1), (0, 1), (2, 0), (-1, -1), (-1, 1), (1, -1), (1, 1), (2, -1), (2, 1), (0, 2), (-1, 2), (1, 2), (2, 2)]

    def mover(own_ref, full, send, recv, part, first_is_x):
        def dev(da, db, core):
            dx, dy = (da, db) if first_is_x else (db, da)
            return at_dev(seq_of(wrap(x + dx), wrap(y + dy), core), z)

        def slot(da, db):
            dx, dy = (da, db) if first_is_x else (db, da)
            return seq_of(wrap(x + dx), wrap(y + dy), c)

        sends = []
        state = [0]

        def recv_id(da, db, hi):
            da, db = (da + 1) % 4, (db + 1) % 4
            return (da * 4 + db) * 2 + hi

        def push(src, dst, target, rsem):
            d = pltpu.make_async_remote_copy(
                src_ref=src, dst_ref=dst, send_sem=send.at[state[0]], recv_sem=rsem, device_id=target, device_id_type=MESH
            )
            state[0] += 1
            d.start()
            sends.append(d)

        def await_(ref, sem):
            pltpu.make_async_copy(ref, ref, sem).wait()

        lo, hi = pl.ds(0, 128), pl.ds(128, 128)

        def step(da, db):
            sl = slot(da, db)
            dst = full.at[sl]
            src = own_ref if (da, db) == (0, 0) else dst
            if (da, db) != (0, 0):
                if da == 2 and db == 0 or db == 2:
                    await_(full.at[sl, lo], recv.at[recv_id(da, db, 0)])
                    await_(full.at[sl, hi], recv.at[recv_id(da, db, 1)])
                else:
                    await_(dst, recv.at[recv_id(da, db, 0)])
            if (da, db) == (0, 0):
                push(src, dst, dev(1, 0, c), recv.at[recv_id(-1, 0, 0)])
                push(src, dst, dev(-1, 0, c), recv.at[recv_id(1, 0, 0)])
            if db == 0:
                if da == -1:
                    push(full.at[sl, lo], full.at[sl, lo], dev(1, 0, c), recv.at[recv_id(2, 0, 0)])
                if da == 1:
                    push(full.at[sl, hi], full.at[sl, hi], dev(-1, 0, c), recv.at[recv_id(2, 0, 1)])
                push(src, dst, dev(0, 1, c), recv.at[recv_id(da, -1, 0)])
                push(src, dst, dev(0, -1, c), recv.at[recv_id(da, 1, 0)])
            if db == -1:
                push(full.at[sl, lo], full.at[sl, lo], dev(0, 1, c), recv.at[recv_id(da, 2, 0)])
            if db == 1:
                push(full.at[sl, hi], full.at[sl, hi], dev(0, -1, c), recv.at[recv_id(da, 2, 1)])
            push(src, dst, dev(0, 0, 1 - c), part.at[recv_id(da, db, 0)])

        def finish():
            for da, db in order:
                dx, dy = (da, db) if first_is_x else (db, da)
                sl = seq_of(wrap(x + dx), wrap(y + dy), 1 - c)
                await_(full.at[sl], part.at[recv_id(da, db, 0)])
            for d in sends:
                d.wait_send()

        return step, finish

    kstep, kfin = mover(k, kfull, ksend, krecv, kpart, True)
    vstep, vfin = mover(v, vfull, vsend, vrecv, vpart, False)

    kstep(0, 0)
    vstep(0, 0)

    moves = []
    for i, (h, g, r, ds) in enumerate(dests):
        mine = jnp.logical_and(ds == s, g == z)
        for srcs, buf, snd, rcv in ((qh, qbuf, qsend, qrecv), (gh, gbuf, gsend, grecv)):
            src = srcs.at[g * 5 + h]
            dst = buf.at[r, :, pl.ds(pl.multiple_of(half * 64, 64), 64), :]
            rem = pltpu.make_async_remote_copy(
                src_ref=src, dst_ref=dst, send_sem=snd.at[i], recv_sem=rcv, device_id=at_dev(ds, g), device_id_type=MESH
            )

            @pl.when(mine)
            def _():
                pltpu.make_async_copy(src, dst, rcv).start()

            @pl.when(jnp.logical_not(mine))
            def _():
                rem.start()

            moves.append((mine, rem))

    for da, db in order[1:]:
        kstep(da, db)
        vstep(da, db)
    kfin()
    vfin()
    pltpu.make_async_copy(qbuf, qbuf, qrecv).wait()
    pltpu.make_async_copy(gbuf, gbuf, grecv).wait()
    for mine, rem in moves:

        @pl.when(jnp.logical_not(mine))
        def _():
            rem.wait_send()

    for d in own:
        d.wait()


def gather(qh, gh, k, v):
    bf = jnp.bfloat16
    dma = pltpu.SemaphoreType.DMA
    return pl.pallas_call(
        gather_kernel,
        out_shape=(
            jax.ShapeDtypeStruct((ROUNDS, 2, 128, 128), bf),
            jax.ShapeDtypeStruct((ROUNDS, 2, 128, 128), bf),
            jax.ShapeDtypeStruct((32, 256, 128), bf),
            jax.ShapeDtypeStruct((32, 256, 128), bf),
        ),
        in_specs=[ANY] * 4,
        out_specs=(ANY,) * 4,
        scratch_shapes=[dma((20,)), dma((20,)), dma, dma, dma((40,)), dma((40,)), dma((32,)), dma((32,)), dma((32,)), dma((32,)), dma((2,))],
        compiler_params=pltpu.CompilerParams(collective_id=0, has_side_effects=True),
        name="gather_units",
    )(qh, gh, k, v)


def attn_kernel(doc_s, doc_v, q_ref, g_ref, k_ref, v_ref, dq_ref, dkv_ref, s_scr, p_scr, dk_acc, dv_acc):
    scale = 1.0 / math.sqrt(128)
    c = scale * math.log2(math.e)
    sidx = lax.axis_index("seq")
    dk_acc[...] = jnp.zeros_like(dk_acc)
    dv_acc[...] = jnp.zeros_like(dv_acc)

    def tile(r, _):
        first = (unit_at(r, sidx) // 5) * 128
        last = first + 127
        start_min = doc_s[first]
        start_max = doc_s[last]
        lo = start_min // BK
        hi = last // BK + 1
        fhi = jnp.minimum((first + 1) // BK, hi)
        flo = jnp.minimum(jnp.maximum(lo, (start_max + BK - 1) // BK), hi)
        fhi = jnp.maximum(fhi, flo)
        srow = doc_v[pl.ds(unit_at(r, sidx) // 5, 1), :]
        prow = first + lax.broadcasted_iota(jnp.int32, (1, 128), 1)
        srow = jnp.concatenate([srow, srow], axis=1)
        prow = jnp.concatenate([prow, prow], axis=1)
        q = q_ref[r]
        g = g_ref[r]

        def stats(masked, kb, carry):
            m, l, w = carry
            o = pl.multiple_of(kb * BK, BK)
            s = lax.dot_general(k_ref[pl.ds(o, BK), :], q, NT, preferred_element_type=jnp.float32)
            dp = lax.dot_general(v_ref[pl.ds(o, BK), :], g, NT, preferred_element_type=jnp.float32)
            if masked:
                kp = o + lax.broadcasted_iota(jnp.int32, (BK, 256), 0)
                s = jnp.where((kp >= srow) & (kp <= prow), s, NEG)
            s_scr[pl.ds(o, BK), :] = s
            p_scr[pl.ds(o, BK), :] = dp
            mn = jnp.maximum(m, jnp.max(s, axis=0, keepdims=True))
            a = jnp.exp2((m - mn) * c)
            e = jnp.exp2((s - mn) * c)
            l = l * a + jnp.sum(e, axis=0, keepdims=True)
            w = w * a + jnp.sum(e * dp, axis=0, keepdims=True)
            return mn, l, w

        zero = jnp.zeros((1, 256), jnp.float32)
        carry = (zero + NEG, zero, zero)
        carry = lax.fori_loop(lo, flo, functools.partial(stats, True), carry)
        carry = lax.fori_loop(flo, fhi, functools.partial(stats, False), carry)
        m, l, w = lax.fori_loop(fhi, hi, functools.partial(stats, True), carry)
        shift = m * c + jnp.log2(l)
        delta = w / l

        def grads(kb, acc):
            o = pl.multiple_of(kb * BK, BK)
            rows = pl.ds(o, BK)
            p = jnp.exp2(s_scr[rows, :] * c - shift)
            ds = p * (p_scr[rows, :] - delta)
            p16 = p.astype(jnp.bfloat16)
            d16 = ds.astype(jnp.bfloat16)
            dv_acc[rows, :] += jnp.dot(p16, g, preferred_element_type=jnp.float32)
            dk_acc[rows, :] += jnp.dot(d16, q, preferred_element_type=jnp.float32)
            return acc + lax.dot_general(d16, k_ref[rows, :], TN, preferred_element_type=jnp.float32)

        acc = lax.fori_loop(lo, hi, grads, jnp.zeros((256, 128), jnp.float32))
        dq_ref[r] = (acc * scale).astype(jnp.bfloat16)
        return 0

    lax.fori_loop(0, ROUNDS, tile, 0)
    dkv_ref[0] = (dk_acc[...] * scale).astype(jnp.bfloat16)
    dkv_ref[1] = dv_acc[...].astype(jnp.bfloat16)


def attn(doc, q, g, k, v):
    return pl.pallas_call(
        attn_kernel,
        out_shape=(
            jax.ShapeDtypeStruct((ROUNDS, 256, 128), jnp.bfloat16),
            jax.ShapeDtypeStruct((2, 8192, 128), jnp.bfloat16),
        ),
        in_specs=[pl.BlockSpec(memory_space=pltpu.SMEM), VM, VM, VM, VM, VM],
        out_specs=(VM, VM),
        scratch_shapes=[
            pltpu.VMEM((8192, 256), jnp.float32),
            pltpu.VMEM((8192, 256), jnp.float32),
            pltpu.VMEM((8192, 128), jnp.float32),
            pltpu.VMEM((8192, 128), jnp.float32),
        ],
        compiler_params=pltpu.CompilerParams(vmem_limit_bytes=62 << 20),
        name="attn_grads",
    )(doc, doc.reshape(64, 128), q, g, k, v)


def reduce_kernel(dq, dkv, dqo, kvo, own, part, send1, mid, rl_lo, rl_hi, from_l, from_r, send2, recv2, fin, dqsend, dqrecv, psend, precv, s1, r1, s2, r2, s3, r3, lsem):
    f32, bf = jnp.float32, jnp.bfloat16
    s, z, x, y, c = coords()
    partner = at_dev(seq_of(x, y, 1 - c), z)
    first_x = c == 0
    a0 = jnp.where(first_x, x, y)
    b0 = jnp.where(first_x, y, x)

    def dev(da, db):
        a, b = wrap(a0 + da), wrap(b0 + db)
        return at_dev(seq_of(jnp.where(first_x, a, b), jnp.where(first_x, b, a), c), z)

    units = []
    for r in range(ROUNDS):
        n = unit_at(r, s)
        b = n // 5
        for hf in range(2):
            units.append((r, hf, lax.rem(n, 5), b // 2, 2 * lax.rem(b, 2) + hf))

    barrier = pltpu.get_barrier_semaphore()
    blk = 2 * s + z // 2
    for h in range(5):
        _, ds = unit_dest(5 * blk + h)
        for g in range(4):
            @pl.when(jnp.logical_not(jnp.logical_and(ds == s, g == z)))
            def _():
                pl.semaphore_signal(barrier, inc=1, device_id=at_dev(ds, g), device_id_type=MESH)
    pl.semaphore_signal(barrier, inc=1, device_id=partner, device_id_type=MESH)
    for d in (1, -1):
        pl.semaphore_signal(barrier, inc=1, device_id=dev(d, 0), device_id_type=MESH)
    for d in (1, -1, 2):
        pl.semaphore_signal(barrier, inc=1, device_id=dev(0, d), device_id_type=MESH)
    selfs = jnp.int32(0)
    for r, hf, h, ss, sz in units:
        selfs = selfs + jnp.logical_and(ss == s, sz == z).astype(jnp.int32)
    pl.semaphore_wait(barrier, 26 - selfs)

    quarters = (2, 1, -1, 0)

    def blocks(ref, which, a, b):
        return ref.at[which, jnp.where(first_x, a, b), jnp.where(first_x, b, a)]

    exch = []
    loads = []
    for qi, d in enumerate(quarters):
        a = wrap(a0 + d)
        pa = wrap(b0 + d)
        for b in range(4):
            i = qi * 4 + b
            src = dkv.at[1 - c, jnp.where(first_x, b, pa), jnp.where(first_x, pa, b)]
            cp = pltpu.make_async_remote_copy(
                src_ref=src, dst_ref=part.at[qi, b], send_sem=psend.at[i], recv_sem=precv.at[i], device_id=partner, device_id_type=MESH
            )
            cp.start()
            exch.append(cp)
            ld = pltpu.make_async_copy(blocks(dkv, c, a, b), own.at[qi, b], lsem.at[i])
            ld.start()
            loads.append(ld)

    moves = []
    for i, (r, hf, h, ss, sz) in enumerate(units):
        mine = jnp.logical_and(ss == s, sz == z)
        src = dq.at[r, :, pl.ds(hf * 64, 64), :]
        dst = dqo.at[z * 5 + h]
        rem = pltpu.make_async_remote_copy(
            src_ref=src, dst_ref=dst, send_sem=dqsend.at[i], recv_sem=dqrecv, device_id=at_dev(ss, sz), device_id_type=MESH
        )

        @pl.when(mine)
        def _():
            pltpu.make_async_copy(src, dst, dqrecv).start()

        @pl.when(jnp.logical_not(mine))
        def _():
            rem.start()

        moves.append((mine, rem))

    def chip_sum(qi, b):
        i = qi * 4 + b
        exch[i].wait_recv()
        loads[i].wait()
        return own[qi, b].astype(f32) + part[qi, b].astype(f32)

    def push(src, dst, ss, rs, target):
        cp = pltpu.make_async_remote_copy(src_ref=src, dst_ref=dst, send_sem=ss, recv_sem=rs, device_id=target, device_id_type=MESH)
        cp.start()
        return cp

    for b in range(4):
        send1[0, b] = chip_sum(0, b).astype(bf)
    relay = [
        push(send1.at[0, pl.ds(0, 2)], rl_lo, s1.at[0], r1.at[0], dev(1, 0)),
        push(send1.at[0, pl.ds(2, 2)], rl_hi, s1.at[1], r1.at[1], dev(-1, 0)),
    ]
    for b in (2, 3):
        send1[1, b] = chip_sum(1, b).astype(bf)
    right = [push(send1.at[1, pl.ds(2, 2)], from_l.at[pl.ds(2, 2)], s1.at[2], r1.at[2], dev(1, 0))]
    for b in (0, 1):
        send1[2, b] = chip_sum(2, b).astype(bf)
    left = [push(send1.at[2, pl.ds(0, 2)], from_r.at[pl.ds(0, 2)], s1.at[3], r1.at[3], dev(-1, 0))]
    relay[0].wait_recv()
    for b in (0, 1):
        send1[1, b] = (chip_sum(1, b) + rl_lo[b].astype(f32)).astype(bf)
    right.append(push(send1.at[1, pl.ds(0, 2)], from_l.at[pl.ds(0, 2)], s1.at[4], r1.at[4], dev(1, 0)))
    relay[1].wait_recv()
    for b in (2, 3):
        send1[2, b] = (chip_sum(2, b) + rl_hi[b - 2].astype(f32)).astype(bf)
    left.append(push(send1.at[2, pl.ds(2, 2)], from_r.at[pl.ds(2, 2)], s1.at[5], r1.at[5], dev(-1, 0)))
    for b in range(4):
        mid[b] = chip_sum(3, b)
    for cp in right + left:
        cp.wait_recv()
    stage2 = []
    for j, d in enumerate((2, 1, -1)):
        b = wrap(b0 + d)
        send2[j] = (mid[b] + from_l[b].astype(f32) + from_r[b].astype(f32)).astype(bf)
        stage2.append(push(send2.at[j], recv2.at[j], s2.at[j], r2.at[j], dev(0, d)))
    tot = mid[b0] + from_l[b0].astype(f32) + from_r[b0].astype(f32)
    for cp in stage2:
        cp.wait_recv()
    tot = tot + recv2[0].astype(f32) + recv2[1].astype(f32) + recv2[2].astype(f32)
    fin[...] = tot.astype(bf)
    last = push(fin.at[pl.ds(pl.multiple_of((1 - c) * 256, 256), 256)], kvo.at[c], s3, r3, partner)
    keep = pltpu.make_async_copy(fin.at[pl.ds(pl.multiple_of(c * 256, 256), 256)], kvo.at[c], lsem.at[16])
    keep.start()

    for cp in relay + right + left + stage2 + exch:
        cp.wait_send()
    last.wait_send()
    pltpu.make_async_copy(fin.at[pl.ds(0, 256)], kvo.at[1 - c], r3).wait()
    keep.wait()
    pltpu.make_async_copy(dqo, dqo, dqrecv).wait()
    for mine, rem in moves:

        @pl.when(jnp.logical_not(mine))
        def _():
            rem.wait_send()


def reduce(dq, dkv):
    bf, f32 = jnp.bfloat16, jnp.float32
    dma = pltpu.SemaphoreType.DMA
    vm = pltpu.VMEM
    return pl.pallas_call(
        reduce_kernel,
        out_shape=(
            jax.ShapeDtypeStruct((20, 2, 64, 128), bf),
            jax.ShapeDtypeStruct((2, 256, 128), bf),
        ),
        in_specs=[ANY] * 2,
        out_specs=(ANY,) * 2,
        scratch_shapes=[
            vm((4, 4, 512, 128), bf), vm((4, 4, 512, 128), bf), vm((3, 4, 512, 128), bf), vm((4, 512, 128), f32),
            vm((2, 512, 128), bf), vm((2, 512, 128), bf), vm((4, 512, 128), bf), vm((4, 512, 128), bf),
            vm((3, 512, 128), bf), vm((3, 512, 128), bf), vm((512, 128), bf),
            dma((20,)), dma, dma((16,)), dma((16,)), dma((6,)), dma((6,)), dma((3,)), dma((3,)), dma, dma, dma((17,)),
        ],
        compiler_params=pltpu.CompilerParams(collective_id=1, has_side_effects=True),
        name="reduce_grads",
    )(dq, dkv)


def per_device(queries, grad_out, keys, values, doc_start):
    qh = jnp.transpose(queries, (2, 0, 1, 3))
    gh = jnp.transpose(grad_out, (2, 0, 1, 3))
    qbuf, gbuf, kfull, vfull = gather(qh, gh, keys.reshape(256, 128), values.reshape(256, 128))
    dq, dkv = attn(
        doc_start,
        qbuf.reshape(ROUNDS, 256, 128),
        gbuf.reshape(ROUNDS, 256, 128),
        kfull.reshape(8192, 128),
        vfull.reshape(8192, 128),
    )
    dqo, kvo = reduce(dq.reshape(ROUNDS, 2, 128, 128), dkv.reshape(2, 4, 4, 512, 128))
    query_grads = jnp.transpose(dqo, (1, 2, 0, 3))
    return query_grads, kvo[0].reshape(256, 1, 128), kvo[1].reshape(256, 1, 128)


def solution(mesh):
    in_specs = (
        P(None, ("seq", "head"), None, None),
        P(None, ("seq", "head"), None, None),
        P("seq", "head", None),
        P("seq", "head", None),
        P(),
    )
    out_specs = (
        P(None, ("seq", "head"), None, None),
        P("seq", "head", None),
        P("seq", "head", None),
    )
    return jax.shard_map(per_device, mesh=mesh, in_specs=in_specs, out_specs=out_specs, check_vma=False)
```

```python
import functools
import math

import jax
import jax.numpy as jnp
from jax import lax
from jax.experimental import pallas as pl
from jax.experimental.pallas import tpu as pltpu
from jax.sharding import PartitionSpec as P

NEG = -1e30
ROUNDS = 10
BK = 1024
CH = 256
FIRST, PACE = 2, 2
MESH = pl.DeviceIdType.MESH
NT = (((1,), (1,)), ((), ()))
TN = (((0,), (0,)), ((), ()))
ANY = pl.BlockSpec(memory_space=pl.ANY)
VM = pl.BlockSpec(memory_space=pltpu.VMEM)


def coords():
    s = lax.axis_index("seq")
    z = lax.axis_index("head")
    c = lax.rem(s, 2)
    y = lax.rem(s // 2, 4)
    x = s // 8
    return s, z, x, y, c


def seq_of(x, y, c):
    return (x * 4 + y) * 2 + c


def wrap(v):
    return lax.rem(v + 4, 4)


def unit_dest(n):
    r = n // 32
    p = lax.rem(n, 32)
    p = jnp.where(lax.rem(r, 2) == 0, p, 31 - p)
    return r, seq_of(lax.rem(p, 4), lax.rem(p // 4, 4), p // 16)


def unit_at(r, s):
    p = s // 8 + 4 * lax.rem(s // 2, 4) + 16 * lax.rem(s, 2)
    return 32 * r + jnp.where(lax.rem(r, 2) == 0, p, 31 - p)


def at_dev(s, z):
    return {"seq": s, "head": z}


def gather_kernel(qh, gh, k, v, qbuf, gbuf, kfull, vfull, qsend, gsend, qrecv, grecv, ksend, vsend, krecv, vrecv, kpart, vpart, lsem):
    s, z, x, y, c = coords()
    half = lax.rem(z, 2)
    blk = 2 * s + z // 2
    dests = []
    for h in range(5):
        r, ds = unit_dest(5 * blk + h)
        for g in range(4):
            dests.append((h, g, r, ds))
    sources = []
    for r in range(ROUNDS):
        b = unit_at(r, s) // 5
        for hf in range(2):
            sources.append((b // 2, 2 * lax.rem(b, 2) + hf))

    barrier = pltpu.get_barrier_semaphore()
    selfs = jnp.int32(0)
    for ss, sz in sources:
        mine = jnp.logical_and(ss == s, sz == z)

        @pl.when(jnp.logical_not(mine))
        def _():
            pl.semaphore_signal(barrier, inc=1, device_id=at_dev(ss, sz), device_id_type=MESH)

        selfs = selfs + mine.astype(jnp.int32)
    ring = [(1, 0), (-1, 0), (0, 1), (0, -1)]
    for dx, dy in ring:
        pl.semaphore_signal(barrier, inc=1, device_id=at_dev(seq_of(wrap(x + dx), wrap(y + dy), c), z), device_id_type=MESH)
    pl.semaphore_signal(barrier, inc=1, device_id=at_dev(seq_of(x, y, 1 - c), z), device_id_type=MESH)
    pl.semaphore_wait(barrier, 25 - selfs)

    own = [
        pltpu.make_async_copy(k, kfull.at[s], lsem.at[0]),
        pltpu.make_async_copy(v, vfull.at[s], lsem.at[1]),
    ]
    for d in own:
        d.start()

    order = [(0, 0), (-1, 0), (1, 0), (0, -1), (0, 1), (2, 0), (-1, -1), (-1, 1), (1, -1), (1, 1), (2, -1), (2, 1), (0, 2), (-1, 2), (1, 2), (2, 2)]

    def mover(own_ref, full, send, recv, part, first_is_x):
        def dev(da, db, core):
            dx, dy = (da, db) if first_is_x else (db, da)
            return at_dev(seq_of(wrap(x + dx), wrap(y + dy), core), z)

        def slot(da, db):
            dx, dy = (da, db) if first_is_x else (db, da)
            return seq_of(wrap(x + dx), wrap(y + dy), c)

        sends = []
        state = [0]

        def recv_id(da, db, hi):
            da, db = (da + 1) % 4, (db + 1) % 4
            return (da * 4 + db) * 2 + hi

        def push(src, dst, target, rsem):
            d = pltpu.make_async_remote_copy(
                src_ref=src, dst_ref=dst, send_sem=send.at[state[0]], recv_sem=rsem, device_id=target, device_id_type=MESH
            )
            state[0] += 1
            d.start()
            sends.append(d)

        def await_(ref, sem):
            pltpu.make_async_copy(ref, ref, sem).wait()

        lo, hi = pl.ds(0, 128), pl.ds(128, 128)

        def step(da, db):
            sl = slot(da, db)
            dst = full.at[sl]
            src = own_ref if (da, db) == (0, 0) else dst
            if (da, db) != (0, 0):
                if da == 2 and db == 0 or db == 2:
                    await_(full.at[sl, lo], recv.at[recv_id(da, db, 0)])
                    await_(full.at[sl, hi], recv.at[recv_id(da, db, 1)])
                else:
                    await_(dst, recv.at[recv_id(da, db, 0)])
            if (da, db) == (0, 0):
                push(src, dst, dev(1, 0, c), recv.at[recv_id(-1, 0, 0)])
                push(src, dst, dev(-1, 0, c), recv.at[recv_id(1, 0, 0)])
            if db == 0:
                if da == -1:
                    push(full.at[sl, lo], full.at[sl, lo], dev(1, 0, c), recv.at[recv_id(2, 0, 0)])
                if da == 1:
                    push(full.at[sl, hi], full.at[sl, hi], dev(-1, 0, c), recv.at[recv_id(2, 0, 1)])
                push(src, dst, dev(0, 1, c), recv.at[recv_id(da, -1, 0)])
                push(src, dst, dev(0, -1, c), recv.at[recv_id(da, 1, 0)])
            if db == -1:
                push(full.at[sl, lo], full.at[sl, lo], dev(0, 1, c), recv.at[recv_id(da, 2, 0)])
            if db == 1:
                push(full.at[sl, hi], full.at[sl, hi], dev(0, -1, c), recv.at[recv_id(da, 2, 1)])
            push(src, dst, dev(0, 0, 1 - c), part.at[recv_id(da, db, 0)])

        def finish():
            for da, db in order:
                dx, dy = (da, db) if first_is_x else (db, da)
                sl = seq_of(wrap(x + dx), wrap(y + dy), 1 - c)
                await_(full.at[sl], part.at[recv_id(da, db, 0)])
            for d in sends:
                d.wait_send()

        return step, finish

    kstep, kfin = mover(k, kfull, ksend, krecv, kpart, True)
    vstep, vfin = mover(v, vfull, vsend, vrecv, vpart, False)

    kstep(0, 0)
    vstep(0, 0)

    moves = []

    def unit_move(i):
        h, g, r, ds = dests[i]
        mine = jnp.logical_and(ds == s, g == z)
        for srcs, buf, snd, rcv in ((qh, qbuf, qsend, qrecv), (gh, gbuf, gsend, grecv)):
            src = srcs.at[g * 5 + h]
            dst = buf.at[r, :, pl.ds(pl.multiple_of(half * 64, 64), 64), :]
            rem = pltpu.make_async_remote_copy(
                src_ref=src, dst_ref=dst, send_sem=snd.at[i], recv_sem=rcv, device_id=at_dev(ds, g), device_id_type=MESH
            )

            @pl.when(mine)
            def _():
                pltpu.make_async_copy(src, dst, rcv).start()

            @pl.when(jnp.logical_not(mine))
            def _():
                rem.start()

            moves.append((mine, rem))

    nxt = 0
    for j, (da, db) in enumerate(order[1:]):
        while nxt < min(20, FIRST + j * PACE):
            unit_move(nxt)
            nxt += 1
        kstep(da, db)
        vstep(da, db)
    kfin()
    vfin()
    pltpu.make_async_copy(qbuf, qbuf, qrecv).wait()
    pltpu.make_async_copy(gbuf, gbuf, grecv).wait()
    for mine, rem in moves:

        @pl.when(jnp.logical_not(mine))
        def _():
            rem.wait_send()

    for d in own:
        d.wait()


def gather(qh, gh, k, v):
    bf = jnp.bfloat16
    dma = pltpu.SemaphoreType.DMA
    return pl.pallas_call(
        gather_kernel,
        out_shape=(
            jax.ShapeDtypeStruct((ROUNDS, 2, 128, 128), bf),
            jax.ShapeDtypeStruct((ROUNDS, 2, 128, 128), bf),
            jax.ShapeDtypeStruct((32, 256, 128), bf),
            jax.ShapeDtypeStruct((32, 256, 128), bf),
        ),
        in_specs=[ANY, ANY, VM, VM],
        out_specs=(ANY,) * 4,
        scratch_shapes=[dma((20,)), dma((20,)), dma, dma, dma((40,)), dma((40,)), dma((32,)), dma((32,)), dma((32,)), dma((32,)), dma((2,))],
        compiler_params=pltpu.CompilerParams(collective_id=0, has_side_effects=True),
        name="gather_units",
    )(qh, gh, k, v)


def attn_kernel(doc_s, doc_v, q_ref, g_ref, k_ref, v_ref, dq_ref, dkv_ref, s_scr, p_scr, dk_acc, dv_acc):
    f32, bf = jnp.float32, jnp.bfloat16
    scale = 1.0 / math.sqrt(128)
    c = scale * math.log2(math.e)
    sidx = lax.axis_index("seq")

    def zero(i, _):
        rows = pl.ds(pl.multiple_of(i * 256, 256), 256)
        dk_acc[rows, :] = jnp.zeros((256, 128), f32)
        dv_acc[rows, :] = jnp.zeros((256, 128), f32)
        return 0

    lax.fori_loop(0, 32, zero, 0)

    def split(x):
        return x.reshape(CH // 8, 8, 256)

    def tile(r, _):
        b = unit_at(r, sidx) // 5
        first = b * 128
        last = first + 127
        start_max = doc_s[last]
        lo = doc_s[first] // BK
        hi = last // BK + 1
        flo = jnp.clip((start_max + BK - 1) // BK, lo + 1, hi)
        fhi = jnp.clip((first + 1) // BK, flo, hi)
        srow = doc_v[pl.ds(b, 1), :]
        prow = first + lax.broadcasted_iota(jnp.int32, (1, 128), 1)
        srow = jnp.concatenate([srow, srow], axis=1)
        prow = jnp.concatenate([prow, prow], axis=1)
        q = q_ref[r]
        g = g_ref[r]

        def produce(masked, o, j, mx):
            start = pl.multiple_of(o + j * CH, CH)
            rows = pl.ds(start, CH)
            s = lax.dot_general(k_ref[rows, :], q, NT, preferred_element_type=f32)
            dp = lax.dot_general(v_ref[rows, :], g, NT, preferred_element_type=f32)
            if masked:
                kp = start + lax.broadcasted_iota(jnp.int32, (CH, 256), 0)
                s = jnp.where((kp >= srow) & (kp <= prow), s, NEG)
            s_scr[rows, :] = s
            p_scr[rows, :] = dp
            return jnp.maximum(mx, jnp.max(split(s), axis=0))

        def consume(o, j, mn, l, w):
            rows = pl.ds(pl.multiple_of(o + j * CH, CH), CH)
            e = jnp.exp2((split(s_scr[rows, :]) - mn) * c)
            return l + jnp.sum(e, axis=0), w + jnp.sum(e * split(p_scr[rows, :]), axis=0)

        neg = jnp.full((8, 256), NEG, f32)
        zeros = jnp.zeros((8, 256), f32)
        mx = neg
        for j in range(BK // CH):
            mx = produce(True, lo * BK, j, mx)

        def body(masked, kb, carry):
            m, l, w, mx = carry
            a = jnp.exp2((m - mx) * c)
            l, w = l * a, w * a
            nx = mx
            o = pl.multiple_of(kb * BK, BK)
            for j in range(BK // CH):
                l, w = consume(o - BK, j, mx, l, w)
                nx = produce(masked, o, j, nx)
            return mx, l, w, nx

        carry = (neg, zeros, zeros, mx)
        carry = lax.fori_loop(lo + 1, flo, functools.partial(body, True), carry)
        carry = lax.fori_loop(flo, fhi, functools.partial(body, False), carry)
        m, l, w, mx = lax.fori_loop(fhi, hi, functools.partial(body, True), carry)
        a = jnp.exp2((m - mx) * c)
        l, w = l * a, w * a
        for j in range(BK // CH):
            l, w = consume((hi - 1) * BK, j, mx, l, w)
        top = jnp.max(mx, axis=0, keepdims=True)
        a = jnp.exp2((mx - top) * c)
        l = jnp.sum(l * a, axis=0, keepdims=True)
        w = jnp.sum(w * a, axis=0, keepdims=True)
        shift = jnp.broadcast_to(top * c + jnp.log2(l), (8, 256))
        delta = jnp.broadcast_to(w / l, (8, 256))

        def grads(kb, acc):
            for j in range(BK // CH):
                rows = pl.ds(pl.multiple_of(kb * BK + j * CH, CH), CH)
                p = jnp.exp2(split(s_scr[rows, :]) * c - shift)
                ds = p * (split(p_scr[rows, :]) - delta)
                p16 = p.reshape(CH, 256).astype(bf)
                d16 = ds.reshape(CH, 256).astype(bf)
                dv_acc[rows, :] += jnp.dot(p16, g, preferred_element_type=f32)
                dk_acc[rows, :] += jnp.dot(d16, q, preferred_element_type=f32)
                acc = acc + lax.dot_general(d16, k_ref[rows, :], TN, preferred_element_type=f32)
            return acc

        acc = lax.fori_loop(lo, hi, grads, jnp.zeros((256, 128), f32))
        dq_ref[r] = (acc * scale).astype(bf)
        return 0

    lax.fori_loop(0, ROUNDS, tile, 0)

    def put(i, _):
        rows = pl.ds(pl.multiple_of(i * 256, 256), 256)
        dkv_ref[0, rows, :] = (dk_acc[rows, :] * scale).astype(bf)
        dkv_ref[1, rows, :] = dv_acc[rows, :].astype(bf)
        return 0

    lax.fori_loop(0, 32, put, 0)


def attn(doc, q, g, k, v):
    return pl.pallas_call(
        attn_kernel,
        out_shape=(
            jax.ShapeDtypeStruct((ROUNDS, 256, 128), jnp.bfloat16),
            jax.ShapeDtypeStruct((2, 8192, 128), jnp.bfloat16),
        ),
        in_specs=[pl.BlockSpec(memory_space=pltpu.SMEM), VM, VM, VM, VM, VM],
        out_specs=(VM, VM),
        scratch_shapes=[
            pltpu.VMEM((8192, 256), jnp.float32),
            pltpu.VMEM((8192, 256), jnp.float32),
            pltpu.VMEM((8192, 128), jnp.float32),
            pltpu.VMEM((8192, 128), jnp.float32),
        ],
        compiler_params=pltpu.CompilerParams(vmem_limit_bytes=62 << 20),
        name="attn_grads",
    )(doc, doc.reshape(64, 128), q, g, k, v)


def reduce_kernel(dq, dkv, dqo, kvo, own, part, send1, mid, rl_lo, rl_hi, from_l, from_r, send2, recv2, fin, dqsend, dqrecv, psend, precv, s1, r1, s2, r2, s3, r3, lsem):
    f32, bf = jnp.float32, jnp.bfloat16
    s, z, x, y, c = coords()
    partner = at_dev(seq_of(x, y, 1 - c), z)
    first_x = c == 0
    a0 = jnp.where(first_x, x, y)
    b0 = jnp.where(first_x, y, x)

    def dev(da, db):
        a, b = wrap(a0 + da), wrap(b0 + db)
        return at_dev(seq_of(jnp.where(first_x, a, b), jnp.where(first_x, b, a), c), z)

    units = []
    for r in range(ROUNDS):
        n = unit_at(r, s)
        b = n // 5
        for hf in range(2):
            units.append((r, hf, lax.rem(n, 5), b // 2, 2 * lax.rem(b, 2) + hf))

    barrier = pltpu.get_barrier_semaphore()
    blk = 2 * s + z // 2
    for h in range(5):
        _, ds = unit_dest(5 * blk + h)
        for g in range(4):
            @pl.when(jnp.logical_not(jnp.logical_and(ds == s, g == z)))
            def _():
                pl.semaphore_signal(barrier, inc=1, device_id=at_dev(ds, g), device_id_type=MESH)
    pl.semaphore_signal(barrier, inc=1, device_id=partner, device_id_type=MESH)
    for d in (1, -1):
        pl.semaphore_signal(barrier, inc=1, device_id=dev(d, 0), device_id_type=MESH)
    for d in (1, -1, 2):
        pl.semaphore_signal(barrier, inc=1, device_id=dev(0, d), device_id_type=MESH)
    selfs = jnp.int32(0)
    for r, hf, h, ss, sz in units:
        selfs = selfs + jnp.logical_and(ss == s, sz == z).astype(jnp.int32)
    pl.semaphore_wait(barrier, 26 - selfs)

    quarters = (2, 1, -1, 0)

    def blocks(ref, which, a, b):
        return ref.at[which, jnp.where(first_x, a, b), jnp.where(first_x, b, a)]

    exch = []
    loads = []
    for qi, d in enumerate(quarters):
        a = wrap(a0 + d)
        pa = wrap(b0 + d)
        for b in range(4):
            i = qi * 4 + b
            src = dkv.at[1 - c, jnp.where(first_x, b, pa), jnp.where(first_x, pa, b)]
            cp = pltpu.make_async_remote_copy(
                src_ref=src, dst_ref=part.at[qi, b], send_sem=psend.at[i], recv_sem=precv.at[i], device_id=partner, device_id_type=MESH
            )
            cp.start()
            exch.append(cp)
            ld = pltpu.make_async_copy(blocks(dkv, c, a, b), own.at[qi, b], lsem.at[i])
            ld.start()
            loads.append(ld)

    moves = []
    for i, (r, hf, h, ss, sz) in enumerate(units):
        mine = jnp.logical_and(ss == s, sz == z)
        src = dq.at[r, :, pl.ds(hf * 64, 64), :]
        dst = dqo.at[z * 5 + h]
        rem = pltpu.make_async_remote_copy(
            src_ref=src, dst_ref=dst, send_sem=dqsend.at[i], recv_sem=dqrecv, device_id=at_dev(ss, sz), device_id_type=MESH
        )

        @pl.when(mine)
        def _():
            pltpu.make_async_copy(src, dst, dqrecv).start()

        @pl.when(jnp.logical_not(mine))
        def _():
            rem.start()

        moves.append((mine, rem))

    def chip_sum(qi, b):
        i = qi * 4 + b
        exch[i].wait_recv()
        loads[i].wait()
        return own[qi, b].astype(f32) + part[qi, b].astype(f32)

    def push(src, dst, ss, rs, target):
        cp = pltpu.make_async_remote_copy(src_ref=src, dst_ref=dst, send_sem=ss, recv_sem=rs, device_id=target, device_id_type=MESH)
        cp.start()
        return cp

    for b in range(4):
        send1[0, b] = chip_sum(0, b).astype(bf)
    relay = [
        push(send1.at[0, pl.ds(0, 2)], rl_lo, s1.at[0], r1.at[0], dev(1, 0)),
        push(send1.at[0, pl.ds(2, 2)], rl_hi, s1.at[1], r1.at[1], dev(-1, 0)),
    ]
    for b in (2, 3):
        send1[1, b] = chip_sum(1, b).astype(bf)
    right = [push(send1.at[1, pl.ds(2, 2)], from_l.at[pl.ds(2, 2)], s1.at[2], r1.at[2], dev(1, 0))]
    for b in (0, 1):
        send1[2, b] = chip_sum(2, b).astype(bf)
    left = [push(send1.at[2, pl.ds(0, 2)], from_r.at[pl.ds(0, 2)], s1.at[3], r1.at[3], dev(-1, 0))]
    relay[0].wait_recv()
    for b in (0, 1):
        send1[1, b] = (chip_sum(1, b) + rl_lo[b].astype(f32)).astype(bf)
    right.append(push(send1.at[1, pl.ds(0, 2)], from_l.at[pl.ds(0, 2)], s1.at[4], r1.at[4], dev(1, 0)))
    relay[1].wait_recv()
    for b in (2, 3):
        send1[2, b] = (chip_sum(2, b) + rl_hi[b - 2].astype(f32)).astype(bf)
    left.append(push(send1.at[2, pl.ds(2, 2)], from_r.at[pl.ds(2, 2)], s1.at[5], r1.at[5], dev(-1, 0)))
    for b in range(4):
        mid[b] = chip_sum(3, b)
    for cp in right + left:
        cp.wait_recv()
    stage2 = []
    for j, d in enumerate((2, 1, -1)):
        b = wrap(b0 + d)
        send2[j] = (mid[b] + from_l[b].astype(f32) + from_r[b].astype(f32)).astype(bf)
        stage2.append(push(send2.at[j], recv2.at[j], s2.at[j], r2.at[j], dev(0, d)))
    tot = mid[b0] + from_l[b0].astype(f32) + from_r[b0].astype(f32)
    for cp in stage2:
        cp.wait_recv()
    tot = tot + recv2[0].astype(f32) + recv2[1].astype(f32) + recv2[2].astype(f32)
    fin[...] = tot.astype(bf)
    last = push(fin.at[pl.ds(pl.multiple_of((1 - c) * 256, 256), 256)], kvo.at[c], s3, r3, partner)
    keep = pltpu.make_async_copy(fin.at[pl.ds(pl.multiple_of(c * 256, 256), 256)], kvo.at[c], lsem.at[16])
    keep.start()

    for cp in relay + right + left + stage2 + exch:
        cp.wait_send()
    last.wait_send()
    pltpu.make_async_copy(fin.at[pl.ds(0, 256)], kvo.at[1 - c], r3).wait()
    keep.wait()
    pltpu.make_async_copy(dqo, dqo, dqrecv).wait()
    for mine, rem in moves:

        @pl.when(jnp.logical_not(mine))
        def _():
            rem.wait_send()


def reduce(dq, dkv):
    bf, f32 = jnp.bfloat16, jnp.float32
    dma = pltpu.SemaphoreType.DMA
    vm = pltpu.VMEM
    return pl.pallas_call(
        reduce_kernel,
        out_shape=(
            jax.ShapeDtypeStruct((20, 2, 64, 128), bf),
            jax.ShapeDtypeStruct((2, 256, 128), bf),
        ),
        in_specs=[ANY] * 2,
        out_specs=(ANY,) * 2,
        scratch_shapes=[
            vm((4, 4, 512, 128), bf), vm((4, 4, 512, 128), bf), vm((3, 4, 512, 128), bf), vm((4, 512, 128), f32),
            vm((2, 512, 128), bf), vm((2, 512, 128), bf), vm((4, 512, 128), bf), vm((4, 512, 128), bf),
            vm((3, 512, 128), bf), vm((3, 512, 128), bf), vm((512, 128), bf),
            dma((20,)), dma, dma((16,)), dma((16,)), dma((6,)), dma((6,)), dma((3,)), dma((3,)), dma, dma, dma((17,)),
        ],
        compiler_params=pltpu.CompilerParams(collective_id=1, has_side_effects=True),
        name="reduce_grads",
    )(dq, dkv)


def per_device(queries, grad_out, keys, values, doc_start):
    qh = jnp.transpose(queries, (2, 0, 1, 3))
    gh = jnp.transpose(grad_out, (2, 0, 1, 3))
    qbuf, gbuf, kfull, vfull = gather(qh, gh, keys.reshape(256, 128), values.reshape(256, 128))
    dq, dkv = attn(
        doc_start,
        qbuf.reshape(ROUNDS, 256, 128),
        gbuf.reshape(ROUNDS, 256, 128),
        kfull.reshape(8192, 128),
        vfull.reshape(8192, 128),
    )
    dqo, kvo = reduce(dq.reshape(ROUNDS, 2, 128, 128), dkv.reshape(2, 4, 4, 512, 128))
    query_grads = jnp.transpose(dqo, (1, 2, 0, 3))
    return query_grads, kvo[0].reshape(256, 1, 128), kvo[1].reshape(256, 1, 128)


def solution(mesh):
    in_specs = (
        P(None, ("seq", "head"), None, None),
        P(None, ("seq", "head"), None, None),
        P("seq", "head", None),
        P("seq", "head", None),
        P(),
    )
    out_specs = (
        P(None, ("seq", "head"), None, None),
        P("seq", "head", None),
        P("seq", "head", None),
    )
    return jax.shard_map(per_device, mesh=mesh, in_specs=in_specs, out_specs=out_specs, check_vma=False)
```

```python
import functools
import math

import jax
import jax.numpy as jnp
from jax import lax
from jax.experimental import pallas as pl
from jax.experimental.pallas import tpu as pltpu
from jax.sharding import PartitionSpec as P

NEG = -1e30
ROUNDS = 10
BK = 1024
SB, CH, GC = 256, 64, 128
FIRST, PACE = 2, 2
MESH = pl.DeviceIdType.MESH
NT = (((1,), (1,)), ((), ()))
TN = (((0,), (0,)), ((), ()))
ANY = pl.BlockSpec(memory_space=pl.ANY)
VM = pl.BlockSpec(memory_space=pltpu.VMEM)


def coords():
    s = lax.axis_index("seq")
    z = lax.axis_index("head")
    c = lax.rem(s, 2)
    y = lax.rem(s // 2, 4)
    x = s // 8
    return s, z, x, y, c


def seq_of(x, y, c):
    return (x * 4 + y) * 2 + c


def wrap(v):
    return lax.rem(v + 4, 4)


def unit_dest(n):
    r = n // 32
    p = lax.rem(n, 32)
    p = jnp.where(lax.rem(r, 2) == 0, p, 31 - p)
    return r, seq_of(lax.rem(p, 4), lax.rem(p // 4, 4), p // 16)


def unit_at(r, s):
    p = s // 8 + 4 * lax.rem(s // 2, 4) + 16 * lax.rem(s, 2)
    return 32 * r + jnp.where(lax.rem(r, 2) == 0, p, 31 - p)


def at_dev(s, z):
    return {"seq": s, "head": z}


def gather_kernel(qh, gh, k, v, qbuf, gbuf, kfull, vfull, qsend, gsend, qrecv, grecv, ksend, vsend, krecv, vrecv, kpart, vpart, lsem):
    s, z, x, y, c = coords()
    half = lax.rem(z, 2)
    blk = 2 * s + z // 2
    dests = []
    for h in range(5):
        r, ds = unit_dest(5 * blk + h)
        for g in range(4):
            dests.append((h, g, r, ds))
    sources = []
    for r in range(ROUNDS):
        b = unit_at(r, s) // 5
        for hf in range(2):
            sources.append((b // 2, 2 * lax.rem(b, 2) + hf))

    barrier = pltpu.get_barrier_semaphore()
    selfs = jnp.int32(0)
    for ss, sz in sources:
        mine = jnp.logical_and(ss == s, sz == z)

        @pl.when(jnp.logical_not(mine))
        def _():
            pl.semaphore_signal(barrier, inc=1, device_id=at_dev(ss, sz), device_id_type=MESH)

        selfs = selfs + mine.astype(jnp.int32)
    ring = [(1, 0), (-1, 0), (0, 1), (0, -1)]
    for dx, dy in ring:
        pl.semaphore_signal(barrier, inc=1, device_id=at_dev(seq_of(wrap(x + dx), wrap(y + dy), c), z), device_id_type=MESH)
    pl.semaphore_signal(barrier, inc=1, device_id=at_dev(seq_of(x, y, 1 - c), z), device_id_type=MESH)
    pl.semaphore_wait(barrier, 25 - selfs)

    own = [
        pltpu.make_async_copy(k, kfull.at[s], lsem.at[0]),
        pltpu.make_async_copy(v, vfull.at[s], lsem.at[1]),
    ]
    for d in own:
        d.start()

    order = [(0, 0), (-1, 0), (1, 0), (0, -1), (0, 1), (2, 0), (-1, -1), (-1, 1), (1, -1), (1, 1), (2, -1), (2, 1), (0, 2), (-1, 2), (1, 2), (2, 2)]

    def mover(own_ref, full, send, recv, part, first_is_x):
        def dev(da, db, core):
            dx, dy = (da, db) if first_is_x else (db, da)
            return at_dev(seq_of(wrap(x + dx), wrap(y + dy), core), z)

        def slot(da, db):
            dx, dy = (da, db) if first_is_x else (db, da)
            return seq_of(wrap(x + dx), wrap(y + dy), c)

        sends = []
        state = [0]

        def recv_id(da, db, hi):
            da, db = (da + 1) % 4, (db + 1) % 4
            return (da * 4 + db) * 2 + hi

        def push(src, dst, target, rsem):
            d = pltpu.make_async_remote_copy(
                src_ref=src, dst_ref=dst, send_sem=send.at[state[0]], recv_sem=rsem, device_id=target, device_id_type=MESH
            )
            state[0] += 1
            d.start()
            sends.append(d)

        def await_(ref, sem):
            pltpu.make_async_copy(ref, ref, sem).wait()

        lo, hi = pl.ds(0, 128), pl.ds(128, 128)

        def step(da, db):
            sl = slot(da, db)
            dst = full.at[sl]
            src = own_ref if (da, db) == (0, 0) else dst
            if (da, db) != (0, 0):
                if da == 2 and db == 0 or db == 2:
                    await_(full.at[sl, lo], recv.at[recv_id(da, db, 0)])
                    await_(full.at[sl, hi], recv.at[recv_id(da, db, 1)])
                else:
                    await_(dst, recv.at[recv_id(da, db, 0)])
            if (da, db) == (0, 0):
                push(src, dst, dev(1, 0, c), recv.at[recv_id(-1, 0, 0)])
                push(src, dst, dev(-1, 0, c), recv.at[recv_id(1, 0, 0)])
            if db == 0:
                if da == -1:
                    push(full.at[sl, lo], full.at[sl, lo], dev(1, 0, c), recv.at[recv_id(2, 0, 0)])
                if da == 1:
                    push(full.at[sl, hi], full.at[sl, hi], dev(-1, 0, c), recv.at[recv_id(2, 0, 1)])
                push(src, dst, dev(0, 1, c), recv.at[recv_id(da, -1, 0)])
                push(src, dst, dev(0, -1, c), recv.at[recv_id(da, 1, 0)])
            if db == -1:
                push(full.at[sl, lo], full.at[sl, lo], dev(0, 1, c), recv.at[recv_id(da, 2, 0)])
            if db == 1:
                push(full.at[sl, hi], full.at[sl, hi], dev(0, -1, c), recv.at[recv_id(da, 2, 1)])
            push(src, dst, dev(0, 0, 1 - c), part.at[recv_id(da, db, 0)])

        def finish():
            for da, db in order:
                dx, dy = (da, db) if first_is_x else (db, da)
                sl = seq_of(wrap(x + dx), wrap(y + dy), 1 - c)
                await_(full.at[sl], part.at[recv_id(da, db, 0)])
            for d in sends:
                d.wait_send()

        return step, finish

    kstep, kfin = mover(k, kfull, ksend, krecv, kpart, True)
    vstep, vfin = mover(v, vfull, vsend, vrecv, vpart, False)

    kstep(0, 0)
    vstep(0, 0)

    moves = []

    def unit_move(i):
        h, g, r, ds = dests[i]
        mine = jnp.logical_and(ds == s, g == z)
        for srcs, buf, snd, rcv in ((qh, qbuf, qsend, qrecv), (gh, gbuf, gsend, grecv)):
            src = srcs.at[g * 5 + h]
            dst = buf.at[r, :, pl.ds(pl.multiple_of(half * 64, 64), 64), :]
            rem = pltpu.make_async_remote_copy(
                src_ref=src, dst_ref=dst, send_sem=snd.at[i], recv_sem=rcv, device_id=at_dev(ds, g), device_id_type=MESH
            )

            @pl.when(mine)
            def _():
                pltpu.make_async_copy(src, dst, rcv).start()

            @pl.when(jnp.logical_not(mine))
            def _():
                rem.start()

            moves.append((mine, rem))

    nxt = 0
    for j, (da, db) in enumerate(order[1:]):
        while nxt < min(20, FIRST + j * PACE):
            unit_move(nxt)
            nxt += 1
        kstep(da, db)
        vstep(da, db)
    kfin()
    vfin()
    pltpu.make_async_copy(qbuf, qbuf, qrecv).wait()
    pltpu.make_async_copy(gbuf, gbuf, grecv).wait()
    for mine, rem in moves:

        @pl.when(jnp.logical_not(mine))
        def _():
            rem.wait_send()

    for d in own:
        d.wait()


def gather(qh, gh, k, v):
    bf = jnp.bfloat16
    dma = pltpu.SemaphoreType.DMA
    return pl.pallas_call(
        gather_kernel,
        out_shape=(
            jax.ShapeDtypeStruct((ROUNDS, 2, 128, 128), bf),
            jax.ShapeDtypeStruct((ROUNDS, 2, 128, 128), bf),
            jax.ShapeDtypeStruct((32, 256, 128), bf),
            jax.ShapeDtypeStruct((32, 256, 128), bf),
        ),
        in_specs=[ANY, ANY, VM, VM],
        out_specs=(ANY,) * 4,
        scratch_shapes=[dma((20,)), dma((20,)), dma, dma, dma((40,)), dma((40,)), dma((32,)), dma((32,)), dma((32,)), dma((32,)), dma((2,))],
        compiler_params=pltpu.CompilerParams(collective_id=0, has_side_effects=True),
        name="gather_units",
    )(qh, gh, k, v)


def attn_kernel(doc_s, doc_v, q_ref, g_ref, k_ref, v_ref, dq_ref, dkv_ref, s0, p0, s1, p1, dk_acc, dv_acc):
    f32, bf = jnp.float32, jnp.bfloat16
    scale = 1.0 / math.sqrt(128)
    c = scale * math.log2(math.e)
    sidx = lax.axis_index("seq")
    scratch = ((s0, p0), (s1, p1))
    neg = jnp.full((8, 256), NEG, f32)
    zeros = jnp.zeros((8, 256), f32)

    def zero(i, _):
        rows = pl.ds(pl.multiple_of(i * 256, 256), 256)
        dk_acc[rows, :] = jnp.zeros((256, 128), f32)
        dv_acc[rows, :] = jnp.zeros((256, 128), f32)
        return 0

    lax.fori_loop(0, 32, zero, 0)

    def split(x):
        return x.reshape(x.shape[0] // 8, 8, 256)

    def info(r):
        b = unit_at(r, sidx) // 5
        first = b * 128
        start_max = doc_s[first + 127]
        lo = (doc_s[first] // 128) * 128
        hi = first + 128
        count = (hi - lo + BK - 1) // BK
        base = jnp.maximum(hi - count * BK, 0)
        flo = jnp.clip((start_max - base + BK - 1) // BK, 0, count)
        fhi = jnp.clip((first + 1 - base) // BK, flo, count)
        return b, first, count, base, flo, fhi

    def spans(b, first):
        srow = doc_v[pl.ds(b, 1), :]
        prow = first + lax.broadcasted_iota(jnp.int32, (1, 128), 1)
        return jnp.concatenate([srow, srow], axis=1), jnp.concatenate([prow, prow], axis=1)

    def stats(r, par, base, span, masked, t, carry):
        m, l, w = carry
        s_scr, p_scr = scratch[par]
        o = base + t * BK
        for h in range(BK // SB):
            rows = pl.ds(pl.multiple_of(o + h * SB, 128), SB)
            s = lax.dot_general(k_ref[rows, :], q_ref[r], NT, preferred_element_type=f32)
            dp = lax.dot_general(v_ref[rows, :], g_ref[r], NT, preferred_element_type=f32)
            for j in range(SB // CH):
                part = slice(j * CH, (j + 1) * CH)
                start = pl.multiple_of(o + h * SB + j * CH, CH)
                sj, dj = s[part], dp[part]
                if masked:
                    kp = start + lax.broadcasted_iota(jnp.int32, (CH, 256), 0)
                    sj = jnp.where((kp >= span[0]) & (kp <= span[1]), sj, NEG)
                s_scr[pl.ds(start, CH), :] = sj
                p_scr[pl.ds(start, CH), :] = dj
                sj, dj = split(sj), split(dj)
                top = jnp.maximum(m, jnp.max(sj, axis=0))
                a = jnp.exp2((m - top) * c)
                e = jnp.exp2((sj - top) * c)
                l = l * a + jnp.sum(e, axis=0)
                w = w * a + jnp.sum(e * dj, axis=0)
                m = top
                yield m, l, w

    def finish(carry):
        m, l, w = carry
        top = jnp.max(m, axis=0, keepdims=True)
        a = jnp.exp2((m - top) * c)
        l = jnp.sum(l * a, axis=0, keepdims=True)
        w = jnp.sum(w * a, axis=0, keepdims=True)
        return jnp.broadcast_to(top * c + jnp.log2(l), (8, 256)), jnp.broadcast_to(w / l, (8, 256))

    def grads(r, par, base, fin, t, acc):
        s_scr, p_scr = scratch[par]
        shift, delta = fin
        for j in range(BK // GC):
            rows = pl.ds(pl.multiple_of(base + t * BK + j * GC, 128), GC)
            p = jnp.exp2(split(s_scr[rows, :]) * c - shift)
            ds = p * (split(p_scr[rows, :]) - delta)
            p16 = p.reshape(GC, 256).astype(bf)
            d16 = ds.reshape(GC, 256).astype(bf)
            dv_acc[rows, :] += jnp.dot(p16, g_ref[r], preferred_element_type=f32)
            dk_acc[rows, :] += jnp.dot(d16, q_ref[r], preferred_element_type=f32)
            acc = acc + lax.dot_general(d16, k_ref[rows, :], TN, preferred_element_type=f32)
            yield acc

    def last(steps):
        for out in steps:
            pass
        return out

    def stats_loop(r, par, inf, span, t0, carry):
        def body(t, carry):
            return lax.cond(
                jnp.logical_and(t >= inf[4], t < inf[5]),
                lambda cc: last(stats(r, par, inf[3], span, False, t, cc)),
                lambda cc: last(stats(r, par, inf[3], span, True, t, cc)),
                carry,
            )

        return lax.fori_loop(t0, inf[2], body, carry)

    def step(r, par, fin):
        inf = info(r)
        nxt = jnp.minimum(r + 1, ROUNDS - 1)
        ninf = info(nxt)
        ninf = ninf[:2] + (jnp.where(r + 1 < ROUNDS, ninf[2], 0),) + ninf[3:]
        span = spans(ninf[0], ninf[1])
        both = jnp.minimum(inf[2], ninf[2])

        def body(t, carry):
            def run(masked):
                def go(cc):
                    acc, st = cc
                    side = grads(r, par, inf[3], fin, t, acc)
                    for i, st in enumerate(stats(nxt, 1 - par, ninf[3], span, masked, t, st)):
                        if (i + 1) % (GC // CH) == 0:
                            acc = next(side)
                    return acc, st

                return go

            return lax.cond(jnp.logical_and(t >= ninf[4], t < ninf[5]), run(False), run(True), carry)

        acc, st = lax.fori_loop(0, both, body, (jnp.zeros((256, 128), f32), (neg, zeros, zeros)))
        acc = lax.fori_loop(both, inf[2], lambda t, a: last(grads(r, par, inf[3], fin, t, a)), acc)
        st = stats_loop(nxt, 1 - par, ninf, span, both, st)
        dq_ref[r] = (acc * scale).astype(bf)
        return finish(st)

    inf0 = info(0)
    fin = finish(stats_loop(0, 0, inf0, spans(inf0[0], inf0[1]), 0, (neg, zeros, zeros)))
    lax.fori_loop(0, ROUNDS // 2, lambda i, fin: step(2 * i + 1, 1, step(2 * i, 0, fin)), fin)

    def put(i, _):
        rows = pl.ds(pl.multiple_of(i * 256, 256), 256)
        dkv_ref[0, rows, :] = (dk_acc[rows, :] * scale).astype(bf)
        dkv_ref[1, rows, :] = dv_acc[rows, :].astype(bf)
        return 0

    lax.fori_loop(0, 32, put, 0)


def attn(doc, q, g, k, v):
    return pl.pallas_call(
        attn_kernel,
        out_shape=(
            jax.ShapeDtypeStruct((ROUNDS, 256, 128), jnp.bfloat16),
            jax.ShapeDtypeStruct((2, 8192, 128), jnp.bfloat16),
        ),
        in_specs=[pl.BlockSpec(memory_space=pltpu.SMEM), VM, VM, VM, VM, VM],
        out_specs=(VM, VM),
        scratch_shapes=[pltpu.VMEM((8192, 256), jnp.float32)] * 4 + [pltpu.VMEM((8192, 128), jnp.float32)] * 2,
        compiler_params=pltpu.CompilerParams(vmem_limit_bytes=62 << 20),
        name="attn_grads",
    )(doc, doc.reshape(64, 128), q, g, k, v)


def reduce_kernel(dq, dkv, dqo, kvo, own, part, send1, mid, rl_lo, rl_hi, from_l, from_r, send2, recv2, fin, dqsend, dqrecv, psend, precv, s1, r1, s2, r2, s3, r3, lsem):
    f32, bf = jnp.float32, jnp.bfloat16
    s, z, x, y, c = coords()
    partner = at_dev(seq_of(x, y, 1 - c), z)
    first_x = c == 0
    a0 = jnp.where(first_x, x, y)
    b0 = jnp.where(first_x, y, x)

    def dev(da, db):
        a, b = wrap(a0 + da), wrap(b0 + db)
        return at_dev(seq_of(jnp.where(first_x, a, b), jnp.where(first_x, b, a), c), z)

    units = []
    for r in range(ROUNDS):
        n = unit_at(r, s)
        b = n // 5
        for hf in range(2):
            units.append((r, hf, lax.rem(n, 5), b // 2, 2 * lax.rem(b, 2) + hf))

    barrier = pltpu.get_barrier_semaphore()
    blk = 2 * s + z // 2
    for h in range(5):
        _, ds = unit_dest(5 * blk + h)
        for g in range(4):
            @pl.when(jnp.logical_not(jnp.logical_and(ds == s, g == z)))
            def _():
                pl.semaphore_signal(barrier, inc=1, device_id=at_dev(ds, g), device_id_type=MESH)
    pl.semaphore_signal(barrier, inc=1, device_id=partner, device_id_type=MESH)
    for d in (1, -1):
        pl.semaphore_signal(barrier, inc=1, device_id=dev(d, 0), device_id_type=MESH)
    for d in (1, -1, 2):
        pl.semaphore_signal(barrier, inc=1, device_id=dev(0, d), device_id_type=MESH)
    selfs = jnp.int32(0)
    for r, hf, h, ss, sz in units:
        selfs = selfs + jnp.logical_and(ss == s, sz == z).astype(jnp.int32)
    pl.semaphore_wait(barrier, 26 - selfs)

    quarters = (2, 1, -1, 0)

    def blocks(ref, which, a, b):
        return ref.at[which, jnp.where(first_x, a, b), jnp.where(first_x, b, a)]

    exch = []
    loads = []
    for qi, d in enumerate(quarters):
        a = wrap(a0 + d)
        pa = wrap(b0 + d)
        for b in range(4):
            i = qi * 4 + b
            src = dkv.at[1 - c, jnp.where(first_x, b, pa), jnp.where(first_x, pa, b)]
            cp = pltpu.make_async_remote_copy(
                src_ref=src, dst_ref=part.at[qi, b], send_sem=psend.at[i], recv_sem=precv.at[i], device_id=partner, device_id_type=MESH
            )
            cp.start()
            exch.append(cp)
            ld = pltpu.make_async_copy(blocks(dkv, c, a, b), own.at[qi, b], lsem.at[i])
            ld.start()
            loads.append(ld)

    moves = []
    for i, (r, hf, h, ss, sz) in enumerate(units):
        mine = jnp.logical_and(ss == s, sz == z)
        src = dq.at[r, :, pl.ds(hf * 64, 64), :]
        dst = dqo.at[z * 5 + h]
        rem = pltpu.make_async_remote_copy(
            src_ref=src, dst_ref=dst, send_sem=dqsend.at[i], recv_sem=dqrecv, device_id=at_dev(ss, sz), device_id_type=MESH
        )

        @pl.when(mine)
        def _():
            pltpu.make_async_copy(src, dst, dqrecv).start()

        @pl.when(jnp.logical_not(mine))
        def _():
            rem.start()

        moves.append((mine, rem))

    def chip_sum(qi, b):
        i = qi * 4 + b
        exch[i].wait_recv()
        loads[i].wait()
        return own[qi, b].astype(f32) + part[qi, b].astype(f32)

    def push(src, dst, ss, rs, target):
        cp = pltpu.make_async_remote_copy(src_ref=src, dst_ref=dst, send_sem=ss, recv_sem=rs, device_id=target, device_id_type=MESH)
        cp.start()
        return cp

    for b in range(4):
        send1[0, b] = chip_sum(0, b).astype(bf)
    relay = [
        push(send1.at[0, pl.ds(0, 2)], rl_lo, s1.at[0], r1.at[0], dev(1, 0)),
        push(send1.at[0, pl.ds(2, 2)], rl_hi, s1.at[1], r1.at[1], dev(-1, 0)),
    ]
    for b in (2, 3):
        send1[1, b] = chip_sum(1, b).astype(bf)
    right = [push(send1.at[1, pl.ds(2, 2)], from_l.at[pl.ds(2, 2)], s1.at[2], r1.at[2], dev(1, 0))]
    for b in (0, 1):
        send1[2, b] = chip_sum(2, b).astype(bf)
    left = [push(send1.at[2, pl.ds(0, 2)], from_r.at[pl.ds(0, 2)], s1.at[3], r1.at[3], dev(-1, 0))]
    relay[0].wait_recv()
    for b in (0, 1):
        send1[1, b] = (chip_sum(1, b) + rl_lo[b].astype(f32)).astype(bf)
    right.append(push(send1.at[1, pl.ds(0, 2)], from_l.at[pl.ds(0, 2)], s1.at[4], r1.at[4], dev(1, 0)))
    relay[1].wait_recv()
    for b in (2, 3):
        send1[2, b] = (chip_sum(2, b) + rl_hi[b - 2].astype(f32)).astype(bf)
    left.append(push(send1.at[2, pl.ds(2, 2)], from_r.at[pl.ds(2, 2)], s1.at[5], r1.at[5], dev(-1, 0)))
    for b in range(4):
        mid[b] = chip_sum(3, b)
    for cp in right + left:
        cp.wait_recv()
    stage2 = []
    for j, d in enumerate((2, 1, -1)):
        b = wrap(b0 + d)
        send2[j] = (mid[b] + from_l[b].astype(f32) + from_r[b].astype(f32)).astype(bf)
        stage2.append(push(send2.at[j], recv2.at[j], s2.at[j], r2.at[j], dev(0, d)))
    tot = mid[b0] + from_l[b0].astype(f32) + from_r[b0].astype(f32)
    for cp in stage2:
        cp.wait_recv()
    tot = tot + recv2[0].astype(f32) + recv2[1].astype(f32) + recv2[2].astype(f32)
    fin[...] = tot.astype(bf)
    last = push(fin.at[pl.ds(pl.multiple_of((1 - c) * 256, 256), 256)], kvo.at[c], s3, r3, partner)
    keep = pltpu.make_async_copy(fin.at[pl.ds(pl.multiple_of(c * 256, 256), 256)], kvo.at[c], lsem.at[16])
    keep.start()

    for cp in relay + right + left + stage2 + exch:
        cp.wait_send()
    last.wait_send()
    pltpu.make_async_copy(fin.at[pl.ds(0, 256)], kvo.at[1 - c], r3).wait()
    keep.wait()
    pltpu.make_async_copy(dqo, dqo, dqrecv).wait()
    for mine, rem in moves:

        @pl.when(jnp.logical_not(mine))
        def _():
            rem.wait_send()


def reduce(dq, dkv):
    bf, f32 = jnp.bfloat16, jnp.float32
    dma = pltpu.SemaphoreType.DMA
    vm = pltpu.VMEM
    return pl.pallas_call(
        reduce_kernel,
        out_shape=(
            jax.ShapeDtypeStruct((20, 2, 64, 128), bf),
            jax.ShapeDtypeStruct((2, 256, 128), bf),
        ),
        in_specs=[ANY] * 2,
        out_specs=(ANY,) * 2,
        scratch_shapes=[
            vm((4, 4, 512, 128), bf), vm((4, 4, 512, 128), bf), vm((3, 4, 512, 128), bf), vm((4, 512, 128), f32),
            vm((2, 512, 128), bf), vm((2, 512, 128), bf), vm((4, 512, 128), bf), vm((4, 512, 128), bf),
            vm((3, 512, 128), bf), vm((3, 512, 128), bf), vm((512, 128), bf),
            dma((20,)), dma, dma((16,)), dma((16,)), dma((6,)), dma((6,)), dma((3,)), dma((3,)), dma, dma, dma((17,)),
        ],
        compiler_params=pltpu.CompilerParams(collective_id=1, has_side_effects=True),
        name="reduce_grads",
    )(dq, dkv)


def per_device(queries, grad_out, keys, values, doc_start):
    qh = jnp.transpose(queries, (2, 0, 1, 3))
    gh = jnp.transpose(grad_out, (2, 0, 1, 3))
    qbuf, gbuf, kfull, vfull = gather(qh, gh, keys.reshape(256, 128), values.reshape(256, 128))
    dq, dkv = attn(
        doc_start,
        qbuf.reshape(ROUNDS, 256, 128),
        gbuf.reshape(ROUNDS, 256, 128),
        kfull.reshape(8192, 128),
        vfull.reshape(8192, 128),
    )
    dqo, kvo = reduce(dq.reshape(ROUNDS, 2, 128, 128), dkv.reshape(2, 4, 4, 512, 128))
    query_grads = jnp.transpose(dqo, (1, 2, 0, 3))
    return query_grads, kvo[0].reshape(256, 1, 128), kvo[1].reshape(256, 1, 128)


def solution(mesh):
    in_specs = (
        P(None, ("seq", "head"), None, None),
        P(None, ("seq", "head"), None, None),
        P("seq", "head", None),
        P("seq", "head", None),
        P(),
    )
    out_specs = (
        P(None, ("seq", "head"), None, None),
        P("seq", "head", None),
        P("seq", "head", None),
    )
    return jax.shard_map(per_device, mesh=mesh, in_specs=in_specs, out_specs=out_specs, check_vma=False)
```

```python
import functools
import math

import jax
import jax.numpy as jnp
from jax import lax
from jax.experimental import pallas as pl
from jax.experimental.pallas import tpu as pltpu
from jax.sharding import PartitionSpec as P

NEG = -1e30
ROUNDS = 10
BK = 1024
SB, CH, GC = 128, 64, 128
FIRST, PACE = 2, 2
MESH = pl.DeviceIdType.MESH
NT = (((1,), (1,)), ((), ()))
TN = (((0,), (0,)), ((), ()))
ANY = pl.BlockSpec(memory_space=pl.ANY)
VM = pl.BlockSpec(memory_space=pltpu.VMEM)


def coords():
    s = lax.axis_index("seq")
    z = lax.axis_index("head")
    c = lax.rem(s, 2)
    y = lax.rem(s // 2, 4)
    x = s // 8
    return s, z, x, y, c


def seq_of(x, y, c):
    return (x * 4 + y) * 2 + c


def wrap(v):
    return lax.rem(v + 4, 4)


def unit_dest(n):
    r = n // 32
    p = lax.rem(n, 32)
    p = jnp.where(lax.rem(r, 2) == 0, p, 31 - p)
    return r, seq_of(lax.rem(p, 4), lax.rem(p // 4, 4), p // 16)


def unit_at(r, s):
    p = s // 8 + 4 * lax.rem(s // 2, 4) + 16 * lax.rem(s, 2)
    return 32 * r + jnp.where(lax.rem(r, 2) == 0, p, 31 - p)


def at_dev(s, z):
    return {"seq": s, "head": z}


def gather_kernel(qh, gh, k, v, qbuf, gbuf, kfull, vfull, qsend, gsend, qrecv, grecv, ksend, vsend, krecv, vrecv, kpart, vpart, lsem):
    s, z, x, y, c = coords()
    half = lax.rem(z, 2)
    blk = 2 * s + z // 2
    dests = []
    for h in range(5):
        r, ds = unit_dest(5 * blk + h)
        for g in range(4):
            dests.append((h, g, r, ds))
    sources = []
    for r in range(ROUNDS):
        b = unit_at(r, s) // 5
        for hf in range(2):
            sources.append((b // 2, 2 * lax.rem(b, 2) + hf))

    barrier = pltpu.get_barrier_semaphore()
    selfs = jnp.int32(0)
    for ss, sz in sources:
        mine = jnp.logical_and(ss == s, sz == z)

        @pl.when(jnp.logical_not(mine))
        def _():
            pl.semaphore_signal(barrier, inc=1, device_id=at_dev(ss, sz), device_id_type=MESH)

        selfs = selfs + mine.astype(jnp.int32)
    ring = [(1, 0), (-1, 0), (0, 1), (0, -1)]
    for dx, dy in ring:
        pl.semaphore_signal(barrier, inc=1, device_id=at_dev(seq_of(wrap(x + dx), wrap(y + dy), c), z), device_id_type=MESH)
    pl.semaphore_signal(barrier, inc=1, device_id=at_dev(seq_of(x, y, 1 - c), z), device_id_type=MESH)
    pl.semaphore_wait(barrier, 25 - selfs)

    own = [
        pltpu.make_async_copy(k, kfull.at[s], lsem.at[0]),
        pltpu.make_async_copy(v, vfull.at[s], lsem.at[1]),
    ]
    for d in own:
        d.start()

    order = [(0, 0), (-1, 0), (1, 0), (0, -1), (0, 1), (2, 0), (-1, -1), (-1, 1), (1, -1), (1, 1), (2, -1), (2, 1), (0, 2), (-1, 2), (1, 2), (2, 2)]

    def mover(own_ref, full, send, recv, part, first_is_x):
        def dev(da, db, core):
            dx, dy = (da, db) if first_is_x else (db, da)
            return at_dev(seq_of(wrap(x + dx), wrap(y + dy), core), z)

        def slot(da, db):
            dx, dy = (da, db) if first_is_x else (db, da)
            return seq_of(wrap(x + dx), wrap(y + dy), c)

        sends = []
        state = [0]

        def recv_id(da, db, hi):
            da, db = (da + 1) % 4, (db + 1) % 4
            return (da * 4 + db) * 2 + hi

        def push(src, dst, target, rsem):
            d = pltpu.make_async_remote_copy(
                src_ref=src, dst_ref=dst, send_sem=send.at[state[0]], recv_sem=rsem, device_id=target, device_id_type=MESH
            )
            state[0] += 1
            d.start()
            sends.append(d)

        def await_(ref, sem):
            pltpu.make_async_copy(ref, ref, sem).wait()

        lo, hi = pl.ds(0, 128), pl.ds(128, 128)

        def step(da, db):
            sl = slot(da, db)
            dst = full.at[sl]
            src = own_ref if (da, db) == (0, 0) else dst
            if (da, db) != (0, 0):
                if da == 2 and db == 0 or db == 2:
                    await_(full.at[sl, lo], recv.at[recv_id(da, db, 0)])
                    await_(full.at[sl, hi], recv.at[recv_id(da, db, 1)])
                else:
                    await_(dst, recv.at[recv_id(da, db, 0)])
            if (da, db) == (0, 0):
                push(src, dst, dev(1, 0, c), recv.at[recv_id(-1, 0, 0)])
                push(src, dst, dev(-1, 0, c), recv.at[recv_id(1, 0, 0)])
            if db == 0:
                if da == -1:
                    push(full.at[sl, lo], full.at[sl, lo], dev(1, 0, c), recv.at[recv_id(2, 0, 0)])
                if da == 1:
                    push(full.at[sl, hi], full.at[sl, hi], dev(-1, 0, c), recv.at[recv_id(2, 0, 1)])
                push(src, dst, dev(0, 1, c), recv.at[recv_id(da, -1, 0)])
                push(src, dst, dev(0, -1, c), recv.at[recv_id(da, 1, 0)])
            if db == -1:
                push(full.at[sl, lo], full.at[sl, lo], dev(0, 1, c), recv.at[recv_id(da, 2, 0)])
            if db == 1:
                push(full.at[sl, hi], full.at[sl, hi], dev(0, -1, c), recv.at[recv_id(da, 2, 1)])
            push(src, dst, dev(0, 0, 1 - c), part.at[recv_id(da, db, 0)])

        def finish():
            for da, db in order:
                dx, dy = (da, db) if first_is_x else (db, da)
                sl = seq_of(wrap(x + dx), wrap(y + dy), 1 - c)
                await_(full.at[sl], part.at[recv_id(da, db, 0)])
            for d in sends:
                d.wait_send()

        return step, finish

    kstep, kfin = mover(k, kfull, ksend, krecv, kpart, True)
    vstep, vfin = mover(v, vfull, vsend, vrecv, vpart, False)

    kstep(0, 0)
    vstep(0, 0)

    moves = []

    def unit_move(i):
        h, g, r, ds = dests[i]
        mine = jnp.logical_and(ds == s, g == z)
        for srcs, buf, snd, rcv in ((qh, qbuf, qsend, qrecv), (gh, gbuf, gsend, grecv)):
            src = srcs.at[g * 5 + h]
            dst = buf.at[r, :, pl.ds(pl.multiple_of(half * 64, 64), 64), :]
            rem = pltpu.make_async_remote_copy(
                src_ref=src, dst_ref=dst, send_sem=snd.at[i], recv_sem=rcv, device_id=at_dev(ds, g), device_id_type=MESH
            )

            @pl.when(mine)
            def _():
                pltpu.make_async_copy(src, dst, rcv).start()

            @pl.when(jnp.logical_not(mine))
            def _():
                rem.start()

            moves.append((mine, rem))

    nxt = 0
    for j, (da, db) in enumerate(order[1:]):
        while nxt < min(20, FIRST + j * PACE):
            unit_move(nxt)
            nxt += 1
        kstep(da, db)
        vstep(da, db)
    kfin()
    vfin()
    pltpu.make_async_copy(qbuf, qbuf, qrecv).wait()
    pltpu.make_async_copy(gbuf, gbuf, grecv).wait()
    for mine, rem in moves:

        @pl.when(jnp.logical_not(mine))
        def _():
            rem.wait_send()

    for d in own:
        d.wait()


def gather(qh, gh, k, v):
    bf = jnp.bfloat16
    dma = pltpu.SemaphoreType.DMA
    return pl.pallas_call(
        gather_kernel,
        out_shape=(
            jax.ShapeDtypeStruct((ROUNDS, 2, 128, 128), bf),
            jax.ShapeDtypeStruct((ROUNDS, 2, 128, 128), bf),
            jax.ShapeDtypeStruct((32, 256, 128), bf),
            jax.ShapeDtypeStruct((32, 256, 128), bf),
        ),
        in_specs=[ANY, ANY, VM, VM],
        out_specs=(ANY,) * 4,
        scratch_shapes=[dma((20,)), dma((20,)), dma, dma, dma((40,)), dma((40,)), dma((32,)), dma((32,)), dma((32,)), dma((32,)), dma((2,))],
        compiler_params=pltpu.CompilerParams(collective_id=0, has_side_effects=True),
        name="gather_units",
    )(qh, gh, k, v)


def attn_kernel(doc_s, doc_v, q_hbm, g_hbm, k_hbm, v_hbm, dq_hbm, dkv_hbm, s0, p0, s1, p1, dk_acc, dv_acc, q_ref, g_ref, k_ref, v_ref, dq_ref, dkv_ref, in_sem, out_sem):
    f32, bf = jnp.float32, jnp.bfloat16
    scale = 1.0 / math.sqrt(128)
    c = scale * math.log2(math.e)
    sidx = lax.axis_index("seq")
    scratch = ((s0, p0), (s1, p1))
    neg = jnp.full((8, 256), NEG, f32)
    zeros = jnp.zeros((8, 256), f32)

    first_rows, rest = pl.ds(0, BK), pl.ds(BK, 8192 - BK)
    pairs = ((q_hbm, q_ref), (g_hbm, g_ref), (k_hbm, k_ref), (v_hbm, v_ref))
    early = [(a.at[pl.ds(0, 1)], b.at[pl.ds(0, 1)]) for a, b in pairs[:2]]
    early += [(a.at[first_rows], b.at[first_rows]) for a, b in pairs[2:]]
    late = [(a.at[pl.ds(1, ROUNDS - 1)], b.at[pl.ds(1, ROUNDS - 1)]) for a, b in pairs[:2]]
    late += [(a.at[rest], b.at[rest]) for a, b in pairs[2:]]
    early = [pltpu.make_async_copy(a, b, in_sem.at[i]) for i, (a, b) in enumerate(early)]
    late = [pltpu.make_async_copy(a, b, in_sem.at[4 + i]) for i, (a, b) in enumerate(late)]
    for cp in early + late:
        cp.start()

    def zero(i, _):
        rows = pl.ds(pl.multiple_of(i * 256, 256), 256)
        dk_acc[rows, :] = jnp.zeros((256, 128), f32)
        dv_acc[rows, :] = jnp.zeros((256, 128), f32)
        return 0

    lax.fori_loop(0, 32, zero, 0)

    def split(x):
        return x.reshape(x.shape[0] // 8, 8, 256)

    def info(r):
        b = unit_at(r, sidx) // 5
        first = b * 128
        start_max = doc_s[first + 127]
        lo = (doc_s[first] // 128) * 128
        hi = first + 128
        count = (hi - lo + BK - 1) // BK
        base = jnp.maximum(hi - count * BK, 0)
        flo = jnp.clip((start_max - base + BK - 1) // BK, 0, count)
        fhi = jnp.clip((first + 1 - base) // BK, flo, count)
        return b, first, count, base, flo, fhi

    def spans(b, first):
        srow = doc_v[pl.ds(b, 1), :]
        prow = first + lax.broadcasted_iota(jnp.int32, (1, 128), 1)
        return jnp.concatenate([srow, srow], axis=1), jnp.concatenate([prow, prow], axis=1)

    def stats(r, par, base, span, masked, t, carry):
        m, l, w = carry
        s_scr, p_scr = scratch[par]
        o = base + t * BK
        for h in range(BK // SB):
            rows = pl.ds(pl.multiple_of(o + h * SB, 128), SB)
            s = lax.dot_general(k_ref[rows, :], q_ref[r], NT, preferred_element_type=f32)
            dp = lax.dot_general(v_ref[rows, :], g_ref[r], NT, preferred_element_type=f32)
            for j in range(SB // CH):
                part = slice(j * CH, (j + 1) * CH)
                start = pl.multiple_of(o + h * SB + j * CH, CH)
                sj, dj = s[part], dp[part]
                if masked:
                    kp = start + lax.broadcasted_iota(jnp.int32, (CH, 256), 0)
                    sj = jnp.where((kp >= span[0]) & (kp <= span[1]), sj, NEG)
                s_scr[pl.ds(start, CH), :] = sj
                p_scr[pl.ds(start, CH), :] = dj
                sj, dj = split(sj), split(dj)
                top = jnp.maximum(m, jnp.max(sj, axis=0))
                a = jnp.exp2((m - top) * c)
                e = jnp.exp2((sj - top) * c)
                l = l * a + jnp.sum(e, axis=0)
                w = w * a + jnp.sum(e * dj, axis=0)
                m = top
                yield m, l, w

    def finish(carry):
        m, l, w = carry
        top = jnp.max(m, axis=0, keepdims=True)
        a = jnp.exp2((m - top) * c)
        l = jnp.sum(l * a, axis=0, keepdims=True)
        w = jnp.sum(w * a, axis=0, keepdims=True)
        return jnp.broadcast_to(top * c + jnp.log2(l), (8, 256)), jnp.broadcast_to(w / l, (8, 256))

    def grads(r, par, base, fin, t, acc):
        s_scr, p_scr = scratch[par]
        shift, delta = fin
        for j in range(BK // GC):
            rows = pl.ds(pl.multiple_of(base + t * BK + j * GC, 128), GC)
            p = jnp.exp2(split(s_scr[rows, :]) * c - shift)
            ds = p * (split(p_scr[rows, :]) - delta)
            p16 = p.reshape(GC, 256).astype(bf)
            d16 = ds.reshape(GC, 256).astype(bf)
            dv_acc[rows, :] += jnp.dot(p16, g_ref[r], preferred_element_type=f32)
            dk_acc[rows, :] += jnp.dot(d16, q_ref[r], preferred_element_type=f32)
            acc = acc + lax.dot_general(d16, k_ref[rows, :], TN, preferred_element_type=f32)
            yield acc

    def last(steps):
        for out in steps:
            pass
        return out

    def stats_loop(r, par, inf, span, t0, carry):
        def body(t, carry):
            return lax.cond(
                jnp.logical_and(t >= inf[4], t < inf[5]),
                lambda cc: last(stats(r, par, inf[3], span, False, t, cc)),
                lambda cc: last(stats(r, par, inf[3], span, True, t, cc)),
                carry,
            )

        return lax.fori_loop(t0, inf[2], body, carry)

    def step(r, par, fin):
        inf = info(r)
        nxt = jnp.minimum(r + 1, ROUNDS - 1)
        ninf = info(nxt)
        ninf = ninf[:2] + (jnp.where(r + 1 < ROUNDS, ninf[2], 0),) + ninf[3:]
        span = spans(ninf[0], ninf[1])
        both = jnp.minimum(inf[2], ninf[2])

        def body(t, carry):
            def run(masked):
                def go(cc):
                    acc, st = cc
                    side = grads(r, par, inf[3], fin, t, acc)
                    for i, st in enumerate(stats(nxt, 1 - par, ninf[3], span, masked, t, st)):
                        if (i + 1) % (GC // CH) == 0:
                            acc = next(side)
                    return acc, st

                return go

            return lax.cond(jnp.logical_and(t >= ninf[4], t < ninf[5]), run(False), run(True), carry)

        acc, st = lax.fori_loop(0, both, body, (jnp.zeros((256, 128), f32), (neg, zeros, zeros)))
        acc = lax.fori_loop(both, inf[2], lambda t, a: last(grads(r, par, inf[3], fin, t, a)), acc)
        st = stats_loop(nxt, 1 - par, ninf, span, both, st)
        dq_ref[r] = (acc * scale).astype(bf)
        return finish(st)

    for cp in early:
        cp.wait()
    inf0 = info(0)
    fin = finish(stats_loop(0, 0, inf0, spans(inf0[0], inf0[1]), 0, (neg, zeros, zeros)))
    for cp in late:
        cp.wait()
    lax.fori_loop(0, ROUNDS // 2, lambda i, fin: step(2 * i + 1, 1, step(2 * i, 0, fin)), fin)

    out = [pltpu.make_async_copy(dq_ref, dq_hbm, out_sem.at[8])]
    out[0].start()
    for n in range(8):

        def put(i, _):
            rows = pl.ds(pl.multiple_of(n * 1024 + i * 256, 256), 256)
            dkv_ref[0, rows, :] = (dk_acc[rows, :] * scale).astype(bf)
            dkv_ref[1, rows, :] = dv_acc[rows, :].astype(bf)
            return 0

        lax.fori_loop(0, 4, put, 0)
        rows = pl.ds(n * 1024, 1024)
        out.append(pltpu.make_async_copy(dkv_ref.at[:, rows], dkv_hbm.at[:, rows], out_sem.at[n]))
        out[-1].start()
    for cp in out:
        cp.wait()


def attn(doc, q, g, k, v):
    return pl.pallas_call(
        attn_kernel,
        out_shape=(
            jax.ShapeDtypeStruct((ROUNDS, 256, 128), jnp.bfloat16),
            jax.ShapeDtypeStruct((2, 8192, 128), jnp.bfloat16),
        ),
        in_specs=[pl.BlockSpec(memory_space=pltpu.SMEM), VM, ANY, ANY, ANY, ANY],
        out_specs=(ANY, ANY),
        scratch_shapes=[pltpu.VMEM((8192, 256), jnp.float32)] * 4
        + [pltpu.VMEM((8192, 128), jnp.float32)] * 2
        + [pltpu.VMEM((ROUNDS, 256, 128), jnp.bfloat16)] * 2
        + [pltpu.VMEM((8192, 128), jnp.bfloat16)] * 2
        + [pltpu.VMEM((ROUNDS, 256, 128), jnp.bfloat16), pltpu.VMEM((2, 8192, 128), jnp.bfloat16)]
        + [pltpu.SemaphoreType.DMA((8,)), pltpu.SemaphoreType.DMA((9,))],
        compiler_params=pltpu.CompilerParams(vmem_limit_bytes=62 << 20),
        name="attn_grads",
    )(doc, doc.reshape(64, 128), q, g, k, v)


def reduce_kernel(dq, dkv, dqo, kvo, own, part, send1, mid, rl_lo, rl_hi, from_l, from_r, send2, recv2, fin, dqsend, dqrecv, psend, precv, s1, r1, s2, r2, s3, r3, lsem):
    f32, bf = jnp.float32, jnp.bfloat16
    s, z, x, y, c = coords()
    partner = at_dev(seq_of(x, y, 1 - c), z)
    first_x = c == 0
    a0 = jnp.where(first_x, x, y)
    b0 = jnp.where(first_x, y, x)

    def dev(da, db):
        a, b = wrap(a0 + da), wrap(b0 + db)
        return at_dev(seq_of(jnp.where(first_x, a, b), jnp.where(first_x, b, a), c), z)

    units = []
    for r in range(ROUNDS):
        n = unit_at(r, s)
        b = n // 5
        for hf in range(2):
            units.append((r, hf, lax.rem(n, 5), b // 2, 2 * lax.rem(b, 2) + hf))

    barrier = pltpu.get_barrier_semaphore()
    blk = 2 * s + z // 2
    for h in range(5):
        _, ds = unit_dest(5 * blk + h)
        for g in range(4):
            @pl.when(jnp.logical_not(jnp.logical_and(ds == s, g == z)))
            def _():
                pl.semaphore_signal(barrier, inc=1, device_id=at_dev(ds, g), device_id_type=MESH)
    pl.semaphore_signal(barrier, inc=1, device_id=partner, device_id_type=MESH)
    for d in (1, -1):
        pl.semaphore_signal(barrier, inc=1, device_id=dev(d, 0), device_id_type=MESH)
    for d in (1, -1, 2):
        pl.semaphore_signal(barrier, inc=1, device_id=dev(0, d), device_id_type=MESH)
    selfs = jnp.int32(0)
    for r, hf, h, ss, sz in units:
        selfs = selfs + jnp.logical_and(ss == s, sz == z).astype(jnp.int32)
    pl.semaphore_wait(barrier, 26 - selfs)

    quarters = (2, 1, -1, 0)

    def blocks(ref, which, a, b):
        return ref.at[which, jnp.where(first_x, a, b), jnp.where(first_x, b, a)]

    exch = []
    loads = []
    for qi, d in enumerate(quarters):
        a = wrap(a0 + d)
        pa = wrap(b0 + d)
        for b in range(4):
            i = qi * 4 + b
            src = dkv.at[1 - c, jnp.where(first_x, b, pa), jnp.where(first_x, pa, b)]
            cp = pltpu.make_async_remote_copy(
                src_ref=src, dst_ref=part.at[qi, b], send_sem=psend.at[i], recv_sem=precv.at[i], device_id=partner, device_id_type=MESH
            )
            cp.start()
            exch.append(cp)
            ld = pltpu.make_async_copy(blocks(dkv, c, a, b), own.at[qi, b], lsem.at[i])
            ld.start()
            loads.append(ld)

    moves = []
    for i, (r, hf, h, ss, sz) in enumerate(units):
        mine = jnp.logical_and(ss == s, sz == z)
        src = dq.at[r, :, pl.ds(hf * 64, 64), :]
        dst = dqo.at[z * 5 + h]
        rem = pltpu.make_async_remote_copy(
            src_ref=src, dst_ref=dst, send_sem=dqsend.at[i], recv_sem=dqrecv, device_id=at_dev(ss, sz), device_id_type=MESH
        )

        @pl.when(mine)
        def _():
            pltpu.make_async_copy(src, dst, dqrecv).start()

        @pl.when(jnp.logical_not(mine))
        def _():
            rem.start()

        moves.append((mine, rem))

    def chip_sum(qi, b):
        i = qi * 4 + b
        exch[i].wait_recv()
        loads[i].wait()
        return own[qi, b].astype(f32) + part[qi, b].astype(f32)

    def push(src, dst, ss, rs, target):
        cp = pltpu.make_async_remote_copy(src_ref=src, dst_ref=dst, send_sem=ss, recv_sem=rs, device_id=target, device_id_type=MESH)
        cp.start()
        return cp

    for b in range(4):
        send1[0, b] = chip_sum(0, b).astype(bf)
    relay = [
        push(send1.at[0, pl.ds(0, 2)], rl_lo, s1.at[0], r1.at[0], dev(1, 0)),
        push(send1.at[0, pl.ds(2, 2)], rl_hi, s1.at[1], r1.at[1], dev(-1, 0)),
    ]
    for b in (2, 3):
        send1[1, b] = chip_sum(1, b).astype(bf)
    right = [push(send1.at[1, pl.ds(2, 2)], from_l.at[pl.ds(2, 2)], s1.at[2], r1.at[2], dev(1, 0))]
    for b in (0, 1):
        send1[2, b] = chip_sum(2, b).astype(bf)
    left = [push(send1.at[2, pl.ds(0, 2)], from_r.at[pl.ds(0, 2)], s1.at[3], r1.at[3], dev(-1, 0))]
    relay[0].wait_recv()
    for b in (0, 1):
        send1[1, b] = (chip_sum(1, b) + rl_lo[b].astype(f32)).astype(bf)
    right.append(push(send1.at[1, pl.ds(0, 2)], from_l.at[pl.ds(0, 2)], s1.at[4], r1.at[4], dev(1, 0)))
    relay[1].wait_recv()
    for b in (2, 3):
        send1[2, b] = (chip_sum(2, b) + rl_hi[b - 2].astype(f32)).astype(bf)
    left.append(push(send1.at[2, pl.ds(2, 2)], from_r.at[pl.ds(2, 2)], s1.at[5], r1.at[5], dev(-1, 0)))
    for b in range(4):
        mid[b] = chip_sum(3, b)
    for cp in right + left:
        cp.wait_recv()
    stage2 = []
    for j, d in enumerate((2, 1, -1)):
        b = wrap(b0 + d)
        send2[j] = (mid[b] + from_l[b].astype(f32) + from_r[b].astype(f32)).astype(bf)
        stage2.append(push(send2.at[j], recv2.at[j], s2.at[j], r2.at[j], dev(0, d)))
    tot = mid[b0] + from_l[b0].astype(f32) + from_r[b0].astype(f32)
    for cp in stage2:
        cp.wait_recv()
    tot = tot + recv2[0].astype(f32) + recv2[1].astype(f32) + recv2[2].astype(f32)
    fin[...] = tot.astype(bf)
    last = push(fin.at[pl.ds(pl.multiple_of((1 - c) * 256, 256), 256)], kvo.at[c], s3, r3, partner)
    keep = pltpu.make_async_copy(fin.at[pl.ds(pl.multiple_of(c * 256, 256), 256)], kvo.at[c], lsem.at[16])
    keep.start()

    for cp in relay + right + left + stage2 + exch:
        cp.wait_send()
    last.wait_send()
    pltpu.make_async_copy(fin.at[pl.ds(0, 256)], kvo.at[1 - c], r3).wait()
    keep.wait()
    pltpu.make_async_copy(dqo, dqo, dqrecv).wait()
    for mine, rem in moves:

        @pl.when(jnp.logical_not(mine))
        def _():
            rem.wait_send()


def reduce(dq, dkv):
    bf, f32 = jnp.bfloat16, jnp.float32
    dma = pltpu.SemaphoreType.DMA
    vm = pltpu.VMEM
    return pl.pallas_call(
        reduce_kernel,
        out_shape=(
            jax.ShapeDtypeStruct((20, 2, 64, 128), bf),
            jax.ShapeDtypeStruct((2, 256, 128), bf),
        ),
        in_specs=[ANY] * 2,
        out_specs=(ANY,) * 2,
        scratch_shapes=[
            vm((4, 4, 512, 128), bf), vm((4, 4, 512, 128), bf), vm((3, 4, 512, 128), bf), vm((4, 512, 128), f32),
            vm((2, 512, 128), bf), vm((2, 512, 128), bf), vm((4, 512, 128), bf), vm((4, 512, 128), bf),
            vm((3, 512, 128), bf), vm((3, 512, 128), bf), vm((512, 128), bf),
            dma((20,)), dma, dma((16,)), dma((16,)), dma((6,)), dma((6,)), dma((3,)), dma((3,)), dma, dma, dma((17,)),
        ],
        compiler_params=pltpu.CompilerParams(collective_id=1, has_side_effects=True),
        name="reduce_grads",
    )(dq, dkv)


def per_device(queries, grad_out, keys, values, doc_start):
    qh = jnp.transpose(queries, (2, 0, 1, 3))
    gh = jnp.transpose(grad_out, (2, 0, 1, 3))
    qbuf, gbuf, kfull, vfull = gather(qh, gh, keys.reshape(256, 128), values.reshape(256, 128))
    dq, dkv = attn(
        doc_start,
        qbuf.reshape(ROUNDS, 256, 128),
        gbuf.reshape(ROUNDS, 256, 128),
        kfull.reshape(8192, 128),
        vfull.reshape(8192, 128),
    )
    dqo, kvo = reduce(dq.reshape(ROUNDS, 2, 128, 128), dkv.reshape(2, 4, 4, 512, 128))
    query_grads = jnp.transpose(dqo, (1, 2, 0, 3))
    return query_grads, kvo[0].reshape(256, 1, 128), kvo[1].reshape(256, 1, 128)


def solution(mesh):
    in_specs = (
        P(None, ("seq", "head"), None, None),
        P(None, ("seq", "head"), None, None),
        P("seq", "head", None),
        P("seq", "head", None),
        P(),
    )
    out_specs = (
        P(None, ("seq", "head"), None, None),
        P("seq", "head", None),
        P("seq", "head", None),
    )
    return jax.shard_map(per_device, mesh=mesh, in_specs=in_specs, out_specs=out_specs, check_vma=False)
```

```python
import functools
import math

import jax
import jax.numpy as jnp
from jax import lax
from jax.experimental import pallas as pl
from jax.experimental.pallas import tpu as pltpu
from jax.sharding import PartitionSpec as P

NEG = -1e30
ROUNDS = 10
BK = 1024
SB, CH, GC = 128, 64, 128
FIRST, PACE = 2, 2
MESH = pl.DeviceIdType.MESH
NT = (((1,), (1,)), ((), ()))
TN = (((0,), (0,)), ((), ()))
ANY = pl.BlockSpec(memory_space=pl.ANY)
VM = pl.BlockSpec(memory_space=pltpu.VMEM)


def coords():
    s = lax.axis_index("seq")
    z = lax.axis_index("head")
    c = lax.rem(s, 2)
    y = lax.rem(s // 2, 4)
    x = s // 8
    return s, z, x, y, c


def seq_of(x, y, c):
    return (x * 4 + y) * 2 + c


def wrap(v):
    return lax.rem(v + 4, 4)


def unit_dest(n):
    r = n // 32
    p = lax.rem(n, 32)
    p = jnp.where(lax.rem(r, 2) == 0, p, 31 - p)
    return r, seq_of(lax.rem(p, 4), lax.rem(p // 4, 4), p // 16)


def unit_at(r, s):
    p = s // 8 + 4 * lax.rem(s // 2, 4) + 16 * lax.rem(s, 2)
    return 32 * r + jnp.where(lax.rem(r, 2) == 0, p, 31 - p)


def at_dev(s, z):
    return {"seq": s, "head": z}


def gather_kernel(qh, gh, k, v, qbuf, gbuf, kfull, vfull, qsend, gsend, qrecv, grecv, ksend, vsend, krecv, vrecv, kpart, vpart, lsem):
    s, z, x, y, c = coords()
    half = lax.rem(z, 2)
    blk = 2 * s + z // 2
    dests = []
    for h in range(5):
        r, ds = unit_dest(5 * blk + h)
        for g in range(4):
            dests.append((h, g, r, ds))
    sources = []
    for r in range(ROUNDS):
        b = unit_at(r, s) // 5
        for hf in range(2):
            sources.append((b // 2, 2 * lax.rem(b, 2) + hf))

    barrier = pltpu.get_barrier_semaphore()
    selfs = jnp.int32(0)
    for ss, sz in sources:
        mine = jnp.logical_and(ss == s, sz == z)

        @pl.when(jnp.logical_not(mine))
        def _():
            pl.semaphore_signal(barrier, inc=1, device_id=at_dev(ss, sz), device_id_type=MESH)

        selfs = selfs + mine.astype(jnp.int32)
    ring = [(1, 0), (-1, 0), (0, 1), (0, -1)]
    for dx, dy in ring:
        pl.semaphore_signal(barrier, inc=1, device_id=at_dev(seq_of(wrap(x + dx), wrap(y + dy), c), z), device_id_type=MESH)
    pl.semaphore_signal(barrier, inc=1, device_id=at_dev(seq_of(x, y, 1 - c), z), device_id_type=MESH)
    pl.semaphore_wait(barrier, 25 - selfs)

    own = [
        pltpu.make_async_copy(k, kfull.at[s], lsem.at[0]),
        pltpu.make_async_copy(v, vfull.at[s], lsem.at[1]),
    ]
    for d in own:
        d.start()

    order = [(0, 0), (-1, 0), (1, 0), (0, -1), (0, 1), (2, 0), (-1, -1), (-1, 1), (1, -1), (1, 1), (2, -1), (2, 1), (0, 2), (-1, 2), (1, 2), (2, 2)]

    def mover(own_ref, full, send, recv, part, first_is_x):
        def dev(da, db, core):
            dx, dy = (da, db) if first_is_x else (db, da)
            return at_dev(seq_of(wrap(x + dx), wrap(y + dy), core), z)

        def slot(da, db):
            dx, dy = (da, db) if first_is_x else (db, da)
            return seq_of(wrap(x + dx), wrap(y + dy), c)

        sends = []
        state = [0]

        def recv_id(da, db, hi):
            da, db = (da + 1) % 4, (db + 1) % 4
            return (da * 4 + db) * 2 + hi

        def push(src, dst, target, rsem):
            d = pltpu.make_async_remote_copy(
                src_ref=src, dst_ref=dst, send_sem=send.at[state[0]], recv_sem=rsem, device_id=target, device_id_type=MESH
            )
            state[0] += 1
            d.start()
            sends.append(d)

        def await_(ref, sem):
            pltpu.make_async_copy(ref, ref, sem).wait()

        lo, hi = pl.ds(0, 128), pl.ds(128, 128)

        def step(da, db):
            sl = slot(da, db)
            dst = full.at[sl]
            src = own_ref if (da, db) == (0, 0) else dst
            if (da, db) != (0, 0):
                if da == 2 and db == 0 or db == 2:
                    await_(full.at[sl, lo], recv.at[recv_id(da, db, 0)])
                    await_(full.at[sl, hi], recv.at[recv_id(da, db, 1)])
                else:
                    await_(dst, recv.at[recv_id(da, db, 0)])
            if (da, db) == (0, 0):
                push(src, dst, dev(1, 0, c), recv.at[recv_id(-1, 0, 0)])
                push(src, dst, dev(-1, 0, c), recv.at[recv_id(1, 0, 0)])
            if db == 0:
                if da == -1:
                    push(full.at[sl, lo], full.at[sl, lo], dev(1, 0, c), recv.at[recv_id(2, 0, 0)])
                if da == 1:
                    push(full.at[sl, hi], full.at[sl, hi], dev(-1, 0, c), recv.at[recv_id(2, 0, 1)])
                push(src, dst, dev(0, 1, c), recv.at[recv_id(da, -1, 0)])
                push(src, dst, dev(0, -1, c), recv.at[recv_id(da, 1, 0)])
            if db == -1:
                push(full.at[sl, lo], full.at[sl, lo], dev(0, 1, c), recv.at[recv_id(da, 2, 0)])
            if db == 1:
                push(full.at[sl, hi], full.at[sl, hi], dev(0, -1, c), recv.at[recv_id(da, 2, 1)])
            push(src, dst, dev(0, 0, 1 - c), part.at[recv_id(da, db, 0)])

        def finish():
            for da, db in order:
                dx, dy = (da, db) if first_is_x else (db, da)
                sl = seq_of(wrap(x + dx), wrap(y + dy), 1 - c)
                await_(full.at[sl], part.at[recv_id(da, db, 0)])
            for d in sends:
                d.wait_send()

        return step, finish

    kstep, kfin = mover(k, kfull, ksend, krecv, kpart, True)
    vstep, vfin = mover(v, vfull, vsend, vrecv, vpart, False)

    kstep(0, 0)
    vstep(0, 0)

    moves = []

    def unit_move(i):
        h, g, r, ds = dests[i]
        mine = jnp.logical_and(ds == s, g == z)
        for srcs, buf, snd, rcv in ((qh, qbuf, qsend, qrecv), (gh, gbuf, gsend, grecv)):
            src = srcs.at[g * 5 + h]
            dst = buf.at[r, :, pl.ds(pl.multiple_of(half * 64, 64), 64), :]
            rem = pltpu.make_async_remote_copy(
                src_ref=src, dst_ref=dst, send_sem=snd.at[i], recv_sem=rcv, device_id=at_dev(ds, g), device_id_type=MESH
            )

            @pl.when(mine)
            def _():
                pltpu.make_async_copy(src, dst, rcv).start()

            @pl.when(jnp.logical_not(mine))
            def _():
                rem.start()

            moves.append((mine, rem))

    nxt = 0
    for j, (da, db) in enumerate(order[1:]):
        while nxt < min(20, FIRST + j * PACE):
            unit_move(nxt)
            nxt += 1
        kstep(da, db)
        vstep(da, db)
    kfin()
    vfin()
    pltpu.make_async_copy(qbuf, qbuf, qrecv).wait()
    pltpu.make_async_copy(gbuf, gbuf, grecv).wait()
    for mine, rem in moves:

        @pl.when(jnp.logical_not(mine))
        def _():
            rem.wait_send()

    for d in own:
        d.wait()


def gather(qh, gh, k, v):
    bf = jnp.bfloat16
    dma = pltpu.SemaphoreType.DMA
    return pl.pallas_call(
        gather_kernel,
        out_shape=(
            jax.ShapeDtypeStruct((ROUNDS, 2, 128, 128), bf),
            jax.ShapeDtypeStruct((ROUNDS, 2, 128, 128), bf),
            jax.ShapeDtypeStruct((32, 256, 128), bf),
            jax.ShapeDtypeStruct((32, 256, 128), bf),
        ),
        in_specs=[ANY, ANY, VM, VM],
        out_specs=(ANY,) * 4,
        scratch_shapes=[dma((20,)), dma((20,)), dma, dma, dma((40,)), dma((40,)), dma((32,)), dma((32,)), dma((32,)), dma((32,)), dma((2,))],
        compiler_params=pltpu.CompilerParams(collective_id=0, has_side_effects=True),
        name="gather_units",
    )(qh, gh, k, v)


def attn_kernel(doc_s, doc_v, q_hbm, g_hbm, k_hbm, v_hbm, dq_hbm, dkv_hbm, s0, p0, s1, p1, dk_acc, dv_acc, q_ref, g_ref, k_ref, v_ref, dq_ref, dkv_ref, in_sem, out_sem):
    f32, bf = jnp.float32, jnp.bfloat16
    scale = 1.0 / math.sqrt(128)
    c = scale * math.log2(math.e)
    sidx = lax.axis_index("seq")
    scratch = ((s0, p0), (s1, p1))
    neg = jnp.full((8, 256), NEG, f32)
    zeros = jnp.zeros((8, 256), f32)

    first_rows, rest = pl.ds(0, BK), pl.ds(BK, 8192 - BK)
    pairs = ((q_hbm, q_ref), (g_hbm, g_ref), (k_hbm, k_ref), (v_hbm, v_ref))
    early = [(a.at[pl.ds(0, 1)], b.at[pl.ds(0, 1)]) for a, b in pairs[:2]]
    early += [(a.at[first_rows], b.at[first_rows]) for a, b in pairs[2:]]
    late = [(a.at[pl.ds(1, ROUNDS - 1)], b.at[pl.ds(1, ROUNDS - 1)]) for a, b in pairs[:2]]
    late += [(a.at[rest], b.at[rest]) for a, b in pairs[2:]]
    early = [pltpu.make_async_copy(a, b, in_sem.at[i]) for i, (a, b) in enumerate(early)]
    late = [pltpu.make_async_copy(a, b, in_sem.at[4 + i]) for i, (a, b) in enumerate(late)]
    for cp in early + late:
        cp.start()

    def zero(i, _):
        rows = pl.ds(pl.multiple_of(i * 256, 256), 256)
        dk_acc[rows, :] = jnp.zeros((256, 128), f32)
        dv_acc[rows, :] = jnp.zeros((256, 128), f32)
        return 0

    lax.fori_loop(0, 32, zero, 0)

    def split(x):
        return x.reshape(x.shape[0] // 8, 8, 256)

    def info(r):
        b = unit_at(r, sidx) // 5
        first = b * 128
        start_max = doc_s[first + 127]
        lo = (doc_s[first] // 128) * 128
        hi = first + 128
        count = (hi - lo + BK - 1) // BK
        base = jnp.maximum(hi - count * BK, 0)
        flo = jnp.clip((start_max - base + BK - 1) // BK, 0, count)
        fhi = jnp.clip((first + 1 - base) // BK, flo, count)
        return b, first, count, base, flo, fhi

    def spans(b, first):
        srow = doc_v[pl.ds(b, 1), :]
        prow = first + lax.broadcasted_iota(jnp.int32, (1, 128), 1)
        return jnp.concatenate([srow, srow], axis=1), jnp.concatenate([prow, prow], axis=1)

    def stats(r, par, base, span, masked, t, carry):
        m, l, w = carry
        s_scr, p_scr = scratch[par]
        o = base + t * BK
        for h in range(BK // SB):
            rows = pl.ds(pl.multiple_of(o + h * SB, 128), SB)
            s = lax.dot_general(k_ref[rows, :], q_ref[r], NT, preferred_element_type=f32)
            dp = lax.dot_general(v_ref[rows, :], g_ref[r], NT, preferred_element_type=f32)
            for j in range(SB // CH):
                part = slice(j * CH, (j + 1) * CH)
                start = pl.multiple_of(o + h * SB + j * CH, CH)
                sj, dj = s[part], dp[part]
                if masked:
                    kp = start + lax.broadcasted_iota(jnp.int32, (CH, 256), 0)
                    sj = jnp.where((kp >= span[0]) & (kp <= span[1]), sj, NEG)
                s_scr[pl.ds(start, CH), :] = sj
                p_scr[pl.ds(start, CH), :] = dj
                sj, dj = split(sj), split(dj)
                top = jnp.maximum(m, jnp.max(sj, axis=0))
                a = jnp.exp2((m - top) * c)
                e = jnp.exp2((sj - top) * c)
                l = l * a + jnp.sum(e, axis=0)
                w = w * a + jnp.sum(e * dj, axis=0)
                m = top
                yield m, l, w

    def finish(carry):
        m, l, w = carry
        top = jnp.max(m, axis=0, keepdims=True)
        a = jnp.exp2((m - top) * c)
        l = jnp.sum(l * a, axis=0, keepdims=True)
        w = jnp.sum(w * a, axis=0, keepdims=True)
        return jnp.broadcast_to(top * c + jnp.log2(l), (8, 256)), jnp.broadcast_to(w / l, (8, 256))

    def grads(r, par, base, fin, t, acc):
        s_scr, p_scr = scratch[par]
        shift, delta = fin
        for j in range(BK // GC):
            rows = pl.ds(pl.multiple_of(base + t * BK + j * GC, 128), GC)
            p = jnp.exp2(split(s_scr[rows, :]) * c - shift)
            ds = p * (split(p_scr[rows, :]) - delta)
            p16 = p.reshape(GC, 256).astype(bf)
            d16 = ds.reshape(GC, 256).astype(bf)
            dv_acc[rows, :] += jnp.dot(p16, g_ref[r], preferred_element_type=f32)
            dk_acc[rows, :] += jnp.dot(d16, q_ref[r], preferred_element_type=f32)
            acc = acc + lax.dot_general(d16, k_ref[rows, :], TN, preferred_element_type=f32)
            yield acc

    def last(steps):
        for out in steps:
            pass
        return out

    def stats_loop(r, par, inf, span, t0, carry):
        def body(t, carry):
            return lax.cond(
                jnp.logical_and(t >= inf[4], t < inf[5]),
                lambda cc: last(stats(r, par, inf[3], span, False, t, cc)),
                lambda cc: last(stats(r, par, inf[3], span, True, t, cc)),
                carry,
            )

        return lax.fori_loop(t0, inf[2], body, carry)

    def step(r, par, fin):
        inf = info(r)
        nxt = jnp.minimum(r + 1, ROUNDS - 1)
        ninf = info(nxt)
        ninf = ninf[:2] + (jnp.where(r + 1 < ROUNDS, ninf[2], 0),) + ninf[3:]
        span = spans(ninf[0], ninf[1])
        both = jnp.minimum(inf[2], ninf[2])

        def body(t, carry):
            def run(masked):
                def go(cc):
                    acc, st = cc
                    side = grads(r, par, inf[3], fin, t, acc)
                    for i, st in enumerate(stats(nxt, 1 - par, ninf[3], span, masked, t, st)):
                        if (i + 1) % (GC // CH) == 0:
                            acc = next(side)
                    return acc, st

                return go

            return lax.cond(jnp.logical_and(t >= ninf[4], t < ninf[5]), run(False), run(True), carry)

        acc, st = lax.fori_loop(0, both, body, (jnp.zeros((256, 128), f32), (neg, zeros, zeros)))
        acc = lax.fori_loop(both, inf[2], lambda t, a: last(grads(r, par, inf[3], fin, t, a)), acc)
        st = stats_loop(nxt, 1 - par, ninf, span, both, st)
        dq_ref[r] = (acc * scale).astype(bf)
        return finish(st)

    for cp in early:
        cp.wait()
    inf0 = info(0)
    fin = finish(stats_loop(0, 0, inf0, spans(inf0[0], inf0[1]), 0, (neg, zeros, zeros)))
    for cp in late:
        cp.wait()
    lax.fori_loop(0, ROUNDS // 2, lambda i, fin: step(2 * i + 1, 1, step(2 * i, 0, fin)), fin)

    out = [pltpu.make_async_copy(dq_ref, dq_hbm, out_sem.at[8])]
    out[0].start()
    for n in range(8):

        def put(i, _):
            rows = pl.ds(pl.multiple_of(n * 1024 + i * 256, 256), 256)
            dkv_ref[0, rows, :] = (dk_acc[rows, :] * scale).astype(bf)
            dkv_ref[1, rows, :] = dv_acc[rows, :].astype(bf)
            return 0

        lax.fori_loop(0, 4, put, 0)
        rows = pl.ds(n * 1024, 1024)
        out.append(pltpu.make_async_copy(dkv_ref.at[:, rows], dkv_hbm.at[:, rows], out_sem.at[n]))
        out[-1].start()
    for cp in out:
        cp.wait()


def attn(doc, q, g, k, v):
    return pl.pallas_call(
        attn_kernel,
        out_shape=(
            jax.ShapeDtypeStruct((ROUNDS, 256, 128), jnp.bfloat16),
            jax.ShapeDtypeStruct((2, 8192, 128), jnp.bfloat16),
        ),
        in_specs=[pl.BlockSpec(memory_space=pltpu.SMEM), VM, ANY, ANY, ANY, ANY],
        out_specs=(ANY, ANY),
        scratch_shapes=[pltpu.VMEM((8192, 256), jnp.float32)] * 4
        + [pltpu.VMEM((8192, 128), jnp.float32)] * 2
        + [pltpu.VMEM((ROUNDS, 256, 128), jnp.bfloat16)] * 2
        + [pltpu.VMEM((8192, 128), jnp.bfloat16)] * 2
        + [pltpu.VMEM((ROUNDS, 256, 128), jnp.bfloat16), pltpu.VMEM((2, 8192, 128), jnp.bfloat16)]
        + [pltpu.SemaphoreType.DMA((8,)), pltpu.SemaphoreType.DMA((9,))],
        compiler_params=pltpu.CompilerParams(vmem_limit_bytes=62 << 20),
        name="attn_grads",
    )(doc, doc.reshape(64, 128), q, g, k, v)


def reduce_kernel(dq, dkv, dqo, kvo, own, part, send1, mid, rl_lo, rl_hi, from_l, from_r, send2, recv2, fin, dqsend, dqrecv, psend, precv, s1, r1, s2, r2, s3, r3, lsem):
    f32, bf = jnp.float32, jnp.bfloat16
    s, z, x, y, c = coords()
    partner = at_dev(seq_of(x, y, 1 - c), z)
    first_x = c == 0
    a0 = jnp.where(first_x, x, y)
    b0 = jnp.where(first_x, y, x)

    def dev(da, db):
        a, b = wrap(a0 + da), wrap(b0 + db)
        return at_dev(seq_of(jnp.where(first_x, a, b), jnp.where(first_x, b, a), c), z)

    units = []
    for step in range(ROUNDS):
        r = lax.rem(s + step, ROUNDS)
        n = unit_at(r, s)
        b = n // 5
        for hf in range(2):
            units.append((r, hf, lax.rem(n, 5), b // 2, 2 * lax.rem(b, 2) + hf))

    barrier = pltpu.get_barrier_semaphore()
    blk = 2 * s + z // 2
    for h in range(5):
        _, ds = unit_dest(5 * blk + h)
        for g in range(4):
            @pl.when(jnp.logical_not(jnp.logical_and(ds == s, g == z)))
            def _():
                pl.semaphore_signal(barrier, inc=1, device_id=at_dev(ds, g), device_id_type=MESH)
    pl.semaphore_signal(barrier, inc=1, device_id=partner, device_id_type=MESH)
    for d in (1, -1):
        pl.semaphore_signal(barrier, inc=1, device_id=dev(d, 0), device_id_type=MESH)
    for d in (1, -1, 2):
        pl.semaphore_signal(barrier, inc=1, device_id=dev(0, d), device_id_type=MESH)
    selfs = jnp.int32(0)
    for r, hf, h, ss, sz in units:
        selfs = selfs + jnp.logical_and(ss == s, sz == z).astype(jnp.int32)
    pl.semaphore_wait(barrier, 26 - selfs)

    quarters = (2, 1, -1, 0)

    def blocks(ref, which, a, b):
        return ref.at[which, jnp.where(first_x, a, b), jnp.where(first_x, b, a)]

    exch = []
    loads = []
    for qi, d in enumerate(quarters):
        a = wrap(a0 + d)
        pa = wrap(b0 + d)
        for b in range(4):
            i = qi * 4 + b
            src = dkv.at[1 - c, jnp.where(first_x, b, pa), jnp.where(first_x, pa, b)]
            cp = pltpu.make_async_remote_copy(
                src_ref=src, dst_ref=part.at[qi, b], send_sem=psend.at[i], recv_sem=precv.at[i], device_id=partner, device_id_type=MESH
            )
            cp.start()
            exch.append(cp)
            ld = pltpu.make_async_copy(blocks(dkv, c, a, b), own.at[qi, b], lsem.at[i])
            ld.start()
            loads.append(ld)

    moves = []
    for i, (r, hf, h, ss, sz) in enumerate(units):
        mine = jnp.logical_and(ss == s, sz == z)
        src = dq.at[r, :, pl.ds(hf * 64, 64), :]
        dst = dqo.at[z * 5 + h]
        rem = pltpu.make_async_remote_copy(
            src_ref=src, dst_ref=dst, send_sem=dqsend.at[i], recv_sem=dqrecv, device_id=at_dev(ss, sz), device_id_type=MESH
        )

        @pl.when(mine)
        def _():
            pltpu.make_async_copy(src, dst, dqrecv).start()

        @pl.when(jnp.logical_not(mine))
        def _():
            rem.start()

        moves.append((mine, rem))

    def chip_sum(qi, b):
        i = qi * 4 + b
        exch[i].wait_recv()
        loads[i].wait()
        return own[qi, b].astype(f32) + part[qi, b].astype(f32)

    def push(src, dst, ss, rs, target):
        cp = pltpu.make_async_remote_copy(src_ref=src, dst_ref=dst, send_sem=ss, recv_sem=rs, device_id=target, device_id_type=MESH)
        cp.start()
        return cp

    for b in range(4):
        send1[0, b] = chip_sum(0, b).astype(bf)
    relay = [
        push(send1.at[0, pl.ds(0, 2)], rl_lo, s1.at[0], r1.at[0], dev(1, 0)),
        push(send1.at[0, pl.ds(2, 2)], rl_hi, s1.at[1], r1.at[1], dev(-1, 0)),
    ]
    for b in (2, 3):
        send1[1, b] = chip_sum(1, b).astype(bf)
    right = [push(send1.at[1, pl.ds(2, 2)], from_l.at[pl.ds(2, 2)], s1.at[2], r1.at[2], dev(1, 0))]
    for b in (0, 1):
        send1[2, b] = chip_sum(2, b).astype(bf)
    left = [push(send1.at[2, pl.ds(0, 2)], from_r.at[pl.ds(0, 2)], s1.at[3], r1.at[3], dev(-1, 0))]
    relay[0].wait_recv()
    for b in (0, 1):
        send1[1, b] = (chip_sum(1, b) + rl_lo[b].astype(f32)).astype(bf)
    right.append(push(send1.at[1, pl.ds(0, 2)], from_l.at[pl.ds(0, 2)], s1.at[4], r1.at[4], dev(1, 0)))
    relay[1].wait_recv()
    for b in (2, 3):
        send1[2, b] = (chip_sum(2, b) + rl_hi[b - 2].astype(f32)).astype(bf)
    left.append(push(send1.at[2, pl.ds(2, 2)], from_r.at[pl.ds(2, 2)], s1.at[5], r1.at[5], dev(-1, 0)))
    for b in range(4):
        mid[b] = chip_sum(3, b)
    for cp in right + left:
        cp.wait_recv()
    stage2 = []
    for j, d in enumerate((2, 1, -1)):
        b = wrap(b0 + d)
        send2[j] = (mid[b] + from_l[b].astype(f32) + from_r[b].astype(f32)).astype(bf)
        stage2.append(push(send2.at[j], recv2.at[j], s2.at[j], r2.at[j], dev(0, d)))
    tot = mid[b0] + from_l[b0].astype(f32) + from_r[b0].astype(f32)
    for cp in stage2:
        cp.wait_recv()
    tot = tot + recv2[0].astype(f32) + recv2[1].astype(f32) + recv2[2].astype(f32)
    fin[...] = tot.astype(bf)
    last = push(fin.at[pl.ds(pl.multiple_of((1 - c) * 256, 256), 256)], kvo.at[c], s3, r3, partner)
    keep = pltpu.make_async_copy(fin.at[pl.ds(pl.multiple_of(c * 256, 256), 256)], kvo.at[c], lsem.at[16])
    keep.start()

    for cp in relay + right + left + stage2 + exch:
        cp.wait_send()
    last.wait_send()
    pltpu.make_async_copy(fin.at[pl.ds(0, 256)], kvo.at[1 - c], r3).wait()
    keep.wait()
    pltpu.make_async_copy(dqo, dqo, dqrecv).wait()
    for mine, rem in moves:

        @pl.when(jnp.logical_not(mine))
        def _():
            rem.wait_send()


def reduce(dq, dkv):
    bf, f32 = jnp.bfloat16, jnp.float32
    dma = pltpu.SemaphoreType.DMA
    vm = pltpu.VMEM
    return pl.pallas_call(
        reduce_kernel,
        out_shape=(
            jax.ShapeDtypeStruct((20, 2, 64, 128), bf),
            jax.ShapeDtypeStruct((2, 256, 128), bf),
        ),
        in_specs=[ANY] * 2,
        out_specs=(ANY,) * 2,
        scratch_shapes=[
            vm((4, 4, 512, 128), bf), vm((4, 4, 512, 128), bf), vm((3, 4, 512, 128), bf), vm((4, 512, 128), f32),
            vm((2, 512, 128), bf), vm((2, 512, 128), bf), vm((4, 512, 128), bf), vm((4, 512, 128), bf),
            vm((3, 512, 128), bf), vm((3, 512, 128), bf), vm((512, 128), bf),
            dma((20,)), dma, dma((16,)), dma((16,)), dma((6,)), dma((6,)), dma((3,)), dma((3,)), dma, dma, dma((17,)),
        ],
        compiler_params=pltpu.CompilerParams(collective_id=1, has_side_effects=True),
        name="reduce_grads",
    )(dq, dkv)


def per_device(queries, grad_out, keys, values, doc_start):
    qh = jnp.transpose(queries, (2, 0, 1, 3))
    gh = jnp.transpose(grad_out, (2, 0, 1, 3))
    qbuf, gbuf, kfull, vfull = gather(qh, gh, keys.reshape(256, 128), values.reshape(256, 128))
    dq, dkv = attn(
        doc_start,
        qbuf.reshape(ROUNDS, 256, 128),
        gbuf.reshape(ROUNDS, 256, 128),
        kfull.reshape(8192, 128),
        vfull.reshape(8192, 128),
    )
    dqo, kvo = reduce(dq.reshape(ROUNDS, 2, 128, 128), dkv.reshape(2, 4, 4, 512, 128))
    query_grads = jnp.transpose(dqo, (1, 2, 0, 3))
    return query_grads, kvo[0].reshape(256, 1, 128), kvo[1].reshape(256, 1, 128)


def solution(mesh):
    in_specs = (
        P(None, ("seq", "head"), None, None),
        P(None, ("seq", "head"), None, None),
        P("seq", "head", None),
        P("seq", "head", None),
        P(),
    )
    out_specs = (
        P(None, ("seq", "head"), None, None),
        P("seq", "head", None),
        P("seq", "head", None),
    )
    return jax.shard_map(per_device, mesh=mesh, in_specs=in_specs, out_specs=out_specs, check_vma=False)
```
